32 devices in a mesh: dp: 8 (over y, x, core), seq: 4 (over z).
Axes of the slice: x: 2, y: 2, z: 4, core: 2. Of those that a mesh axis runs over, the one named last changes fastest.
Arguments:
- inputs: bfloat16 [8, 1024, 1024], P('dp', 'seq'), may hold values from -6 to 6
- cotangent: bfloat16 [8, 1024, 1024], P('dp', 'seq'), may hold values from -6 to 6
- query_proj: bfloat16 [1024, 1024], P(('dp', 'seq')), may hold values from -0.1875 to 0.1875
- key_proj: bfloat16 [1024, 1024], P(('dp', 'seq')), may hold values from -0.1875 to 0.1875
- value_proj: bfloat16 [1024, 2048], P(('dp', 'seq')), may hold values from -0.1875 to 0.1875
- gate_proj: bfloat16 [1024, 2048], P(('dp', 'seq')), may hold values from -0.1875 to 0.1875
- rate_proj: bfloat16 [1024, 16], P(('dp', 'seq')), may hold values from -0.1875 to 0.1875
- output_proj: bfloat16 [2048, 1024], P(('dp', 'seq')), may hold values from -0.125 to 0.125
- ffn_gate: bfloat16 [1024, 2816], P(('dp', 'seq')), may hold values from -0.1875 to 0.1875
- ffn_up: bfloat16 [1024, 2816], P(('dp', 'seq')), may hold values from -0.1875 to 0.1875
- ffn_down: bfloat16 [2816, 1024], P(('dp', 'seq')), may hold values from -0.109375 to 0.109375
- mixer_gain: float32 [1024], replicated, may hold values from 0.5 to 1.5
- ffn_gain: float32 [1024], replicated, may hold values from 0.5 to 1.5
- query_filter: float32 [4, 1024], replicated, may hold values from -3 to 3
- key_filter: float32 [4, 1024], replicated, may hold values from -3 to 3
- value_filter: float32 [4, 2048], replicated, may hold values from -3 to 3
- decay_log: float32 [8], replicated, may hold values from 0 to 2.7
- step_bias: float32 [8], replicated, may hold values from -6 to -3
- head_gain: float32 [256], replicated, may hold values from 0.5 to 1.5
Outputs:
- block_out: bfloat16 [8, 1024, 1024], P('dp', 'seq')
- grad_inputs: bfloat16 [8, 1024, 1024], P('dp', 'seq')
- grad_query: bfloat16 [1024, 1024], P(('dp', 'seq'))
- grad_key: bfloat16 [1024, 1024], P(('dp', 'seq'))
- grad_value: bfloat16 [1024, 2048], P(('dp', 'seq'))
- grad_gate: bfloat16 [1024, 2048], P(('dp', 'seq'))
- grad_rate: bfloat16 [1024, 16], P(('dp', 'seq'))
- grad_output: bfloat16 [2048, 1024], P(('dp', 'seq'))
- grad_ffngate: bfloat16 [1024, 2816], P(('dp', 'seq'))
- grad_ffnup: bfloat16 [1024, 2816], P(('dp', 'seq'))
- grad_ffndown: bfloat16 [2816, 1024], P(('dp', 'seq'))
- grad_mixgain: bfloat16 [1024], replicated
- grad_ffngain: bfloat16 [1024], replicated
- grad_qfilter: bfloat16 [4, 1024], replicated
- grad_kfilter: bfloat16 [4, 1024], replicated
- grad_vfilter: bfloat16 [4, 2048], replicated
- grad_decay: bfloat16 [8], replicated
- grad_stepbias: bfloat16 [8], replicated
- grad_headgain: bfloat16 [256], replicated
The draws below stay inside these ranges and needn't reach their ends.
All inputs are finite; a program needn't handle non-finite values.
Results may differ from the reference program's by a relative error of at most 0.019.
Values may be sent and summed in bfloat16 or wider, within the bound.
No kernel may reach another device: no remote copies, remote signals or barrier semaphores. Data moves between devices by JAX's collectives and lax.ppermute only.
A program may use at most 112 MiB of HBM per device.

```python
import jax
import jax.numpy as jnp
from jax import lax

D = 1024
H = 8
DK = 128
DV = 256
FF = 2816
TAPS = 4
BLOCK = 64
LENGTH = 1024
BATCH = 8


def block_levels(own_key, extent, cuts, smallest, top_value):
    loudness, own = 1.0, jax.random.fold_in(own_key, 6)
    for position, blocks in cuts:
        steps = jnp.exp(jax.random.uniform(jax.random.fold_in(own, position), (blocks,), jnp.float32, smallest / len(cuts), top_value / len(cuts)))
        loudness = loudness * jnp.repeat(steps, extent[position] // blocks).reshape([-1 if axis == position else 1 for axis in range(len(extent))])
    return loudness


def bell_draw(own_key, shape, scale, limit, pieces=(), kind=jnp.bfloat16):
    array = jax.random.normal(own_key, shape, jnp.float32) * scale
    if len(pieces) > 0:
        array = block_levels(own_key, shape, pieces, -0.22, 0.18) * array
    return jnp.clip(array, min=-limit, max=limit).astype(kind)


def setup_inputs(seed: int = 0) -> dict:
    streams_of = jax.random.split(jax.random.key(seed), 20)
    inputs = bell_draw(streams_of[0], (BATCH, LENGTH, D), 1.0, 6.0, ((0, 8), (1, 4)))
    cotangent = bell_draw(streams_of[1], (BATCH, LENGTH, D), 1.0, 6.0, ((0, 8), (1, 4)))
    query_proj = bell_draw(streams_of[2], (D, H * DK), D ** -0.5, 0.1875, ((0, 32),))
    key_proj = bell_draw(streams_of[3], (D, H * DK), D ** -0.5, 0.1875, ((0, 32),))
    value_proj = bell_draw(streams_of[4], (D, H * DV), D ** -0.5, 0.1875, ((0, 32),))
    gate_proj = bell_draw(streams_of[5], (D, H * DV), D ** -0.5, 0.1875, ((0, 32),))
    rate_proj = bell_draw(streams_of[6], (D, 2 * H), D ** -0.5, 0.1875, ((0, 32),))
    output_proj = bell_draw(streams_of[7], (H * DV, D), (H * DV) ** -0.5, 0.125, ((0, 32),))
    ffn_gate = bell_draw(streams_of[8], (D, FF), D ** -0.5, 0.1875, ((0, 32),))
    ffn_up = bell_draw(streams_of[9], (D, FF), D ** -0.5, 0.1875, ((0, 32),))
    ffn_down = bell_draw(streams_of[10], (FF, D), FF ** -0.5, 0.109375, ((0, 32),))
    mixer_gain = jnp.clip(1.0 + 0.1 * jax.random.normal(streams_of[11], (D,), jnp.float32), 0.5, 1.5)
    ffn_gain = jnp.clip(1.0 + 0.1 * jax.random.normal(streams_of[12], (D,), jnp.float32), 0.5, 1.5)
    query_filter = bell_draw(streams_of[13], (TAPS, H * DK), TAPS ** -0.5, 3.0, (), jnp.float32)
    key_filter = bell_draw(streams_of[14], (TAPS, H * DK), TAPS ** -0.5, 3.0, (), jnp.float32)
    value_filter = bell_draw(streams_of[15], (TAPS, H * DV), TAPS ** -0.5, 3.0, (), jnp.float32)
    decay_log = jnp.clip(jax.random.uniform(streams_of[16], (H,), jnp.float32, 0.0, 2.7), 0.0, 2.7)
    step_bias = jnp.clip(jax.random.uniform(streams_of[17], (H,), jnp.float32, -6.0, -3.0), -6.0, -3.0)
    head_gain = jnp.clip(1.0 + 0.1 * jax.random.normal(streams_of[18], (DV,), jnp.float32), 0.5, 1.5)
    return {"inputs": inputs, "cotangent": cotangent, "query_proj": query_proj, "key_proj": key_proj, "value_proj": value_proj, "gate_proj": gate_proj, "rate_proj": rate_proj, "output_proj": output_proj, "ffn_gate": ffn_gate, "ffn_up": ffn_up, "ffn_down": ffn_down, "mixer_gain": mixer_gain, "ffn_gain": ffn_gain, "query_filter": query_filter, "key_filter": key_filter, "value_filter": value_filter, "decay_log": decay_log, "step_bias": step_bias, "head_gain": head_gain}


@jax.custom_vjp
def low(v):
    return lax.optimization_barrier(v.astype(jnp.bfloat16)).astype(jnp.float32)

@jax.custom_vjp
def low_back(v):
    return v

def low_keep(v):
    return (low(v), None)

def low_pass(kept, grad):
    return (grad,)

def back_keep(v):
    return (v, None)

def back_low(kept, grad):
    return (low(grad),)
low.defvjp(low_keep, low_pass)
low_back.defvjp(back_keep, back_low)
precise = lax.Precision.HIGHEST
per_group = 4

def matmul_rows(values, weight):
    return jnp.einsum('...i,ij->...j', values, weight, precision=precise)

def rms_scale(values, gain):
    return values * lax.rsqrt(lax.optimization_barrier(jnp.mean(values * values, axis=-1, keepdims=True)) + 1e-05) * gain

def causal_conv(series, filters):
    taps_count = filters.shape[0]
    length_here = series.shape[1]
    padded = jnp.pad(series, ((0, 0), (taps_count - 1, 0), (0, 0), (0, 0)))
    summed = padded[:, 0:length_here] * filters[0]
    for offset in range(1, taps_count):
        summed = summed + padded[:, offset:offset + length_here] * filters[offset]
    return jax.nn.silu(summed)

def to_blocks(series):
    shaped = series.reshape((series.shape[0], series.shape[1] // BLOCK, BLOCK, series.shape[2]) + series.shape[3:])
    return jnp.swapaxes(jnp.moveaxis(shaped, 1, 0), 2, 3)

def from_blocks(blocked):
    moved = jnp.moveaxis(jnp.swapaxes(blocked, 2, 3), 0, 1)
    return moved.reshape((moved.shape[0], moved.shape[1] * BLOCK, moved.shape[3], moved.shape[4]))

def block_step(memory, blocks_in):
    query_part, key_part, value_part, strength_part, decay_part = blocks_in
    running = jnp.cumsum(decay_part, axis=-1)
    row_ids = lax.broadcasted_iota(jnp.int32, (BLOCK, BLOCK), 0)
    col_ids = lax.broadcasted_iota(jnp.int32, (BLOCK, BLOCK), 1)
    lower = row_ids >= col_ids
    strict = row_ids > col_ids
    spread = jnp.where(lower, running[..., :, None] - running[..., None, :], 0.0)
    decays = jnp.where(lower, jnp.exp(spread), 0.0)
    inner = jnp.einsum('bhid,bhjd->bhij', key_part, key_part, precision=precise)
    coupling = jnp.where(strict, strength_part[..., :, None] * inner * decays, 0.0)
    identity = jnp.eye(BLOCK, dtype=coupling.dtype)
    inverse = identity - coupling
    power = coupling
    reach = 2
    while reach < BLOCK:
        power = jnp.einsum('bhij,bhjk->bhik', power, power, precision=precise)
        inverse = jnp.einsum('bhij,bhjk->bhik', inverse, identity + power, precision=precise)
        reach = reach * 2
    scaling = jnp.exp(running)
    carried = jnp.einsum('bhid,bhdv->bhiv', key_part, memory, precision=precise)
    target = strength_part[..., None] * (value_part - scaling[..., None] * carried)
    update = jnp.einsum('bhij,bhjv->bhiv', inverse, target, precision=precise)
    scores = jnp.einsum('bhid,bhjd->bhij', query_part, key_part, precision=precise) * decays
    output = scaling[..., None] * jnp.einsum('bhid,bhdv->bhiv', query_part, memory, precision=precise)
    output = output + jnp.einsum('bhij,bhjv->bhiv', scores, update, precision=precise)
    tail_decay = jnp.exp(running[..., -1:] - running)
    memory = jnp.exp(running[..., -1])[..., None, None] * memory
    memory = memory + jnp.einsum('bhid,bhiv->bhdv', key_part * tail_decay[..., None], update, precision=precise)
    return (memory, output)

def mixer(query_in, key_in, value_in, gate_in, rate_in, query_taps, key_taps, value_taps, decay_log, step_bias, head_gain):
    queries = causal_conv(query_in, query_taps)
    keys = causal_conv(key_in, key_taps)
    values = causal_conv(value_in, value_taps)
    queries = queries * lax.rsqrt(lax.optimization_barrier(jnp.sum(queries * queries, axis=-1, keepdims=True)) + 1e-06) * queries.shape[-1] ** (-0.5)
    keys = keys * lax.rsqrt(lax.optimization_barrier(jnp.sum(keys * keys, axis=-1, keepdims=True)) + 1e-06)
    strength = jax.nn.sigmoid(rate_in[..., 0])
    log_decay = -jnp.exp(decay_log) * jax.nn.softplus(rate_in[..., 1] + step_bias)
    start_state = jnp.zeros((queries.shape[0], queries.shape[2], keys.shape[-1], values.shape[-1]), queries.dtype)
    final_state, blocked = lax.scan(jax.checkpoint(block_step), start_state, (to_blocks(queries), to_blocks(keys), to_blocks(values), to_blocks(strength), to_blocks(log_decay)))
    raw = from_blocks(blocked)
    normal = raw * lax.rsqrt(lax.optimization_barrier(jnp.mean(raw * raw, axis=-1, keepdims=True)) + 1e-05)
    return normal * head_gain * jax.nn.silu(gate_in)

def block(residual, query_proj, key_proj, value_proj, gate_proj, rate_proj, output_proj, ffn_gate, ffn_up, ffn_down, mixer_gain, ffn_gain, query_filter, key_filter, value_filter, decay_log, step_bias, head_gain):
    seq_count = residual.shape[0]
    seq_len = residual.shape[1]
    normed = low(rms_scale(residual, mixer_gain))

    def project(weight, last):
        return low(low_back(matmul_rows(normed, weight))).reshape((seq_count, seq_len, H, last))
    mixed = mixer(project(query_proj, DK), project(key_proj, DK), project(value_proj, DV), project(gate_proj, DV), project(rate_proj, 2), query_filter.reshape(TAPS, H, DK), key_filter.reshape(TAPS, H, DK), value_filter.reshape(TAPS, H, DV), decay_log, step_bias, head_gain)
    mixed = low(low_back(mixed)).reshape(seq_count, seq_len, H * DV)
    middle = residual + low_back(matmul_rows(mixed, output_proj))
    normed_two = low(rms_scale(middle, ffn_gain))
    hidden_gate = low_back(matmul_rows(normed_two, ffn_gate))
    hidden_up = low_back(matmul_rows(normed_two, ffn_up))
    activated = low(jax.nn.silu(hidden_gate) * hidden_up)
    return middle + matmul_rows(activated, ffn_down)

def reference(inputs, cotangent, query_proj, key_proj, value_proj, gate_proj, rate_proj, output_proj, ffn_gate, ffn_up, ffn_down, mixer_gain, ffn_gain, query_filter, key_filter, value_filter, decay_log, step_bias, head_gain):
    params = tuple((member.astype(jnp.float32) for member in (query_proj, key_proj, value_proj, gate_proj, rate_proj, output_proj, ffn_gate, ffn_up, ffn_down, mixer_gain, ffn_gain, query_filter, key_filter, value_filter, decay_log, step_bias, head_gain)))
    group_count = inputs.shape[0] // per_group
    series_in = inputs.astype(jnp.float32).reshape((group_count, per_group) + inputs.shape[1:])
    series_cot = cotangent.astype(jnp.float32).reshape((group_count, per_group) + inputs.shape[1:])

    def one_group(grad_sums, group_pair):
        group_in, group_cot = group_pair
        result, pullback = jax.vjp(block, group_in, *params)
        gradients = pullback(group_cot)
        updated = tuple((running + fresh for running, fresh in zip(grad_sums, gradients[1:])))
        return (updated, (result, gradients[0]))
    grad_sums, (results, input_grads) = lax.scan(one_group, tuple((jnp.zeros_like(member) for member in params)), (series_in, series_cot))
    block_out = results.reshape(inputs.shape).astype(jnp.bfloat16)
    grad_inputs = input_grads.reshape(inputs.shape).astype(jnp.bfloat16)
    finals = tuple((member.astype(jnp.bfloat16) for member in grad_sums))
    return (block_out, grad_inputs, finals[0], finals[1], finals[2], finals[3], finals[4], finals[5], finals[6], finals[7], finals[8], finals[9], finals[10], finals[11], finals[12], finals[13], finals[14], finals[15], finals[16])
```

```python
import functools

import jax
import jax.numpy as jnp
from jax import lax
from jax.experimental import pallas as pl
from jax.experimental.pallas import tpu as pltpu
from jax.sharding import PartitionSpec as P

H = 8
DK = 128
DV = 256


CHUNK = 256
LANES = 128
F32 = jnp.float32
BF16 = jnp.bfloat16


def mm(left, right, left_dim=1, right_dim=0):
    return lax.dot_general(
        left.astype(BF16),
        right.astype(BF16),
        (((left_dim,), (right_dim,)), ((), ())),
        preferred_element_type=F32,
    )


def mm_nt(left, right):
    return mm(left, right, 1, 1)


def mm_tn(left, right):
    return mm(left, right, 0, 0)


def iota(shape, axis):
    return lax.broadcasted_iota(jnp.int32, shape, axis)


def exact_mm(ones, values):
    first = values.astype(BF16)
    rest = values - first.astype(F32)
    second = rest.astype(BF16)
    third = (rest - second.astype(F32)).astype(BF16)
    return mm(ones, first) + mm(ones, second) + mm(ones, third)


def small_inverse(coupling):
    size = coupling.shape[0]
    rows = iota(coupling.shape, 0)
    cols = iota(coupling.shape, 1)
    solved = jnp.where((rows // 2 == cols // 2), -coupling, 0.0)
    width = 2
    while width < size:
        band = (rows // (2 * width) == cols // (2 * width)) & (rows // width != cols // width)
        part = jnp.where(band, coupling, 0.0)
        step = part + mm(part, solved)
        solved = solved - step - mm(solved, step)
        width = 2 * width
    return solved


def lower_inverse(coupling):
    size = coupling.shape[0]
    if size <= LANES:
        return small_inverse(coupling)
    half = size // 2
    head = lower_inverse(coupling[:half, :half])
    tail = lower_inverse(coupling[half:, half:])
    part = coupling[half:, :half]
    step = part + mm(part, head)
    corner = -step - mm(tail, step)
    top = jnp.concatenate([head, jnp.zeros((half, half), F32)], axis=1)
    return jnp.concatenate([top, jnp.concatenate([corner, tail], axis=1)], axis=0)


def silu_slope(values, gate):
    return gate * (1.0 + values * (1.0 - gate))


def softplus(values):
    return jnp.maximum(values, 0.0) + jnp.log1p(jnp.exp(-jnp.abs(values)))


def conv_taps(current, before, first_chunk):
    before = jnp.where(first_chunk, 0.0, before.astype(F32))
    joined = jnp.concatenate([before, current.astype(F32)], axis=0)
    top = before.shape[0]
    rows = current.shape[0]
    return [joined[top - 3 + tap : top - 3 + tap + rows] for tap in range(4)]


def decay_parts(rate, decay_scale, decay_bias):
    rows = rate.shape[0]
    shifted = rate + decay_bias
    log_decay = -decay_scale * softplus(shifted)
    lower = jnp.where(iota((rows, rows), 0) >= iota((rows, rows), 1), 1.0, 0.0)
    running = exact_mm(lower, log_decay)
    return shifted, log_decay, running


def head_parts(summed, running, running_rows, head, heads):
    rows = summed.shape[0]
    gates = jax.nn.sigmoid(summed)
    conv = summed * gates
    q_at, k_at, v_at = head * DK, (heads + head) * DK, 2 * heads * DK + head * DV
    q_conv, k_conv = conv[:, q_at : q_at + DK], conv[:, k_at : k_at + DK]
    value = conv[:, v_at : v_at + DV]
    q_scale = lax.rsqrt(jnp.sum(q_conv * q_conv, axis=1, keepdims=True) + 1e-06)
    k_scale = lax.rsqrt(jnp.sum(k_conv * k_conv, axis=1, keepdims=True) + 1e-06)
    query = q_conv * (q_scale * DK**-0.5)
    key = k_conv * k_scale
    lane = 2 * head + 1
    total = running[:, lane : lane + 1]
    across = running_rows[lane : lane + 1, :]
    lower = iota((rows, rows), 0) >= iota((rows, rows), 1)
    decays = jnp.where(lower, jnp.exp(jnp.minimum(total - across, 0.0)), 0.0)
    last = total[rows - 1 : rows, :]
    return q_conv, k_conv, q_scale, k_scale, query, key, value, total, decays, last


def mixer_forward_kernel(
    current_ref, before_ref, filter_ref, side_ref, gain_ref,
    mixed_ref, solved_ref, update_ref, start_ref, raw_ref, memory_ref, *, heads
):
    chunk = pl.program_id(1)

    @pl.when(chunk == 0)
    def _():
        memory_ref[...] = jnp.zeros(memory_ref.shape, F32)

    conv_width = 2 * heads * DK + heads * DV
    gate_at = conv_width
    rate_at = conv_width + heads * DV
    taps = conv_taps(
        current_ref[0, :, :conv_width], before_ref[0, :, :conv_width], chunk == 0
    )
    rows = taps[0].shape[0]
    summed = taps[0] * filter_ref[0:1, :]
    for tap in range(1, 4):
        summed = summed + taps[tap] * filter_ref[tap : tap + 1, :]
    rate = current_ref[0, :, rate_at : rate_at + LANES].astype(F32)
    strengths = jax.nn.sigmoid(rate)
    shifted, log_decay, running = decay_parts(rate, side_ref[0:1, :], side_ref[1:2, :])
    running_rows = running.T
    strict = iota((rows, rows), 0) > iota((rows, rows), 1)
    for head in range(heads):
        _, _, _, _, query, key, value, total, decays, last = head_parts(
            summed, running, running_rows, head, heads
        )
        strength = strengths[:, 2 * head : 2 * head + 1]
        scaling = jnp.exp(total)
        inner = mm_nt(key, key)
        coupling = jnp.where(strict, strength * inner * decays, 0.0)
        solved = lower_inverse(coupling)
        start = memory_ref[head]
        target = strength * (value - scaling * mm(key, start))
        update = target + mm(solved, target)
        scores = mm_nt(query, key) * decays
        raw = scaling * mm(query, start) + mm(scores, update)
        tail = key * jnp.exp(last - total)
        memory_ref[head] = jnp.exp(last) * start + mm_tn(tail, update)
        start_ref[0, 0, head] = start
        solved_ref[0, 0, head] = solved.astype(BF16)
        at = head * DV
        update_ref[0, :, at : at + DV] = update.astype(BF16)
        raw_ref[0, :, at : at + DV] = raw
        gate = current_ref[0, :, gate_at + at : gate_at + at + DV].astype(F32)
        normal = raw * lax.rsqrt(jnp.mean(raw * raw, axis=1, keepdims=True) + 1e-05)
        mixed_ref[0, :, at : at + DV] = (
            normal * gain_ref[...] * (gate * jax.nn.sigmoid(gate))
        ).astype(BF16)


def mixer_backward_kernel(
    current_ref, before_ref, filter_ref, side_ref, gain_ref,
    adjoint_ref, solved_ref, update_ref, start_ref, raw_ref,
    grad_ref, filter_sum_ref, side_sum_ref, gain_sum_ref, memory_ref, after_ref, *, heads, chunks
):
    step = pl.program_id(1)

    @pl.when(step == 0)
    def _():
        memory_ref[...] = jnp.zeros(memory_ref.shape, F32)
        after_ref[...] = jnp.zeros(after_ref.shape, F32)

    @pl.when((step == 0) & (pl.program_id(0) == 0))
    def _():
        filter_sum_ref[...] = jnp.zeros(filter_sum_ref.shape, F32)
        side_sum_ref[...] = jnp.zeros(side_sum_ref.shape, F32)
        gain_sum_ref[...] = jnp.zeros(gain_sum_ref.shape, F32)

    conv_width = 2 * heads * DK + heads * DV
    gate_at = conv_width
    rate_at = conv_width + heads * DV
    taps = conv_taps(
        current_ref[0, :, :conv_width], before_ref[0, :, :conv_width], step == chunks - 1
    )
    rows = taps[0].shape[0]
    summed = taps[0] * filter_ref[0:1, :]
    for tap in range(1, 4):
        summed = summed + taps[tap] * filter_ref[tap : tap + 1, :]
    rate = current_ref[0, :, rate_at : rate_at + LANES].astype(F32)
    strengths = jax.nn.sigmoid(rate)
    decay_scale = side_ref[0:1, :]
    shifted, log_decay, running = decay_parts(rate, decay_scale, side_ref[1:2, :])
    running_rows = running.T
    strict = iota((rows, rows), 0) > iota((rows, rows), 1)
    lane_ids = iota((rows, LANES), 1)
    row_ids = iota((LANES, rows), 0)
    last_lanes = iota((1, LANES), 1)
    sum_across = jnp.zeros((rows, LANES), F32)
    sum_down = jnp.zeros((LANES, rows), F32)
    sum_last = jnp.zeros((1, LANES), F32)
    adj_strength = jnp.zeros((rows, LANES), F32)
    q_adjoints, k_adjoints, v_adjoints = [], [], []
    for head in range(heads):
        q_conv, k_conv, q_scale, k_scale, query, key, value, total, decays, last = head_parts(
            summed, running, running_rows, head, heads
        )
        strength = strengths[:, 2 * head : 2 * head + 1]
        scaling = jnp.exp(total)
        at = head * DV
        raw = raw_ref[0, :, at : at + DV]
        gate = current_ref[0, :, gate_at + at : gate_at + at + DV].astype(F32)
        gate_sig = jax.nn.sigmoid(gate)
        gate_silu = gate * gate_sig
        adj_mixed = adjoint_ref[0, :, at : at + DV].astype(F32)
        inv = lax.rsqrt(jnp.mean(raw * raw, axis=1, keepdims=True) + 1e-05)
        normal = raw * inv
        upstream = adj_mixed * gain_ref[...] * gate_silu
        adj_raw = inv * (
            upstream - normal * jnp.mean(upstream * normal, axis=1, keepdims=True)
        )
        adj_gate = adj_mixed * normal * gain_ref[...] * silu_slope(gate, gate_sig)
        grad_ref[0, :, gate_at + at : gate_at + at + DV] = adj_gate.astype(BF16)
        gain_sum_ref[...] += jnp.sum(adj_mixed * normal * gate_silu, axis=0, keepdims=True)

        start = start_ref[0, 0, head]
        solved = solved_ref[0, 0, head]
        update = update_ref[0, :, at : at + DV]
        adj_memory = memory_ref[head]
        tail_decay = jnp.exp(last - total)
        last_decay = jnp.exp(last)
        inner = mm_nt(key, key)
        scores = mm_nt(query, key) * decays
        spread = mm(key * tail_decay, adj_memory)
        adj_update = mm_tn(scores, adj_raw) + spread
        adj_target = adj_update + mm_tn(solved, adj_update)
        adj_scores = mm_nt(adj_raw, update)
        adj_coupling = jnp.where(strict, -mm_nt(adj_target, update), 0.0) * decays
        adj_inner = strength * adj_coupling
        from_inner = adj_coupling * inner
        adj_qk = adj_scores * decays
        key_start = mm(key, start)
        query_start = mm(query, start)
        adj_query = scaling * mm_nt(adj_raw, start) + mm(adj_qk, key)
        adj_key = (
            mm_tn(adj_qk, query)
            + tail_decay * mm_nt(update, adj_memory)
            - scaling * strength * mm_nt(adj_target, start)
            + mm(adj_inner, key)
            + mm_tn(adj_inner, key)
        )
        adj_value = strength * adj_target
        strength_sum = jnp.sum(
            adj_target * (value - scaling * key_start), axis=1, keepdims=True
        ) + jnp.sum(from_inner, axis=1, keepdims=True)
        pairs = adj_scores * scores + strength * from_inner
        tail_sum = jnp.sum(spread * update.astype(F32), axis=1, keepdims=True)
        decay_sum = (
            jnp.sum(pairs, axis=1, keepdims=True)
            + scaling * jnp.sum(query_start * adj_raw, axis=1, keepdims=True)
            - scaling * strength * jnp.sum(key_start * adj_target, axis=1, keepdims=True)
            - tail_sum
        )
        at_end = jnp.sum(tail_sum, axis=0, keepdims=True) + last_decay * jnp.sum(
            jnp.sum(start * adj_memory, axis=1, keepdims=True), axis=0, keepdims=True
        )
        lane = 2 * head + 1
        sum_across = sum_across + jnp.where(lane_ids == lane, decay_sum, 0.0)
        sum_down = sum_down + jnp.where(
            row_ids == lane, jnp.sum(pairs, axis=0, keepdims=True), 0.0
        )
        sum_last = sum_last + jnp.where(last_lanes == lane, at_end, 0.0)
        adj_strength = adj_strength + jnp.where(lane_ids == lane - 1, strength_sum, 0.0)
        memory_ref[head] = (
            last_decay * adj_memory
            + mm_tn(query * scaling, adj_raw)
            - mm_tn(key * (scaling * strength), adj_target)
        )
        adj_query = adj_query * DK**-0.5
        q_adjoints.append(
            q_scale * adj_query
            - q_conv
            * (q_scale * q_scale * q_scale * jnp.sum(q_conv * adj_query, axis=1, keepdims=True))
        )
        k_adjoints.append(
            k_scale * adj_key
            - k_conv
            * (k_scale * k_scale * k_scale * jnp.sum(k_conv * adj_key, axis=1, keepdims=True))
        )
        v_adjoints.append(adj_value)

    upper = jnp.where(iota((rows, rows), 0) <= iota((rows, rows), 1), 1.0, 0.0)
    adj_log_decay = exact_mm(upper, sum_across - sum_down.T) + sum_last
    adj_shifted = -adj_log_decay * decay_scale * jax.nn.sigmoid(shifted)
    adj_rate = adj_shifted + adj_strength * strengths * (1.0 - strengths)
    grad_ref[0, :, rate_at : rate_at + LANES] = adj_rate.astype(BF16)
    side_sum_ref[0:1, :] += jnp.sum(adj_log_decay * log_decay, axis=0, keepdims=True)
    side_sum_ref[1:2, :] += jnp.sum(adj_shifted, axis=0, keepdims=True)

    adj_conv = jnp.concatenate(q_adjoints + k_adjoints + v_adjoints, axis=1)
    adj_summed = adj_conv * silu_slope(summed, jax.nn.sigmoid(summed))
    joined = jnp.concatenate([adj_summed, after_ref[...]], axis=0)
    after_ref[...] = adj_summed[0:8]
    adj_pre = adj_summed * filter_ref[3:4, :]
    filter_sum_ref[3:4, :] += jnp.sum(adj_summed * taps[3], axis=0, keepdims=True)
    for tap in range(3):
        adj_pre = adj_pre + joined[3 - tap : 3 - tap + rows] * filter_ref[tap : tap + 1, :]
        filter_sum_ref[tap : tap + 1, :] += jnp.sum(adj_summed * taps[tap], axis=0, keepdims=True)
    grad_ref[0, :, :conv_width] = adj_pre.astype(BF16)


def mixer_sizes(projected, heads):
    seqs, tokens, width = projected.shape
    rows = min(CHUNK, tokens)
    conv_width = 2 * heads * DK + heads * DV
    return seqs, tokens, width, rows, tokens // rows, conv_width


def mixer_forward(projected, filters, side, gain, heads):
    seqs, tokens, width, rows, chunks, conv_width = mixer_sizes(projected, heads)
    ratio = rows // 16
    per_row = lambda s, c: (s, c, 0)
    fixed = lambda s, c: (0, 0)
    per_chunk = lambda s, c: (s, c, 0, 0, 0)
    return pl.pallas_call(
        functools.partial(mixer_forward_kernel, heads=heads),
        grid=(seqs, chunks),
        in_specs=[
            pl.BlockSpec((1, rows, width), per_row),
            pl.BlockSpec((1, 16, width), lambda s, c: (s, jnp.maximum(c * ratio - 1, 0), 0)),
            pl.BlockSpec((4, conv_width), fixed),
            pl.BlockSpec((8, LANES), fixed),
            pl.BlockSpec((1, DV), fixed),
        ],
        out_specs=[
            pl.BlockSpec((1, rows, heads * DV), per_row),
            pl.BlockSpec((1, 1, heads, rows, rows), per_chunk),
            pl.BlockSpec((1, rows, heads * DV), per_row),
            pl.BlockSpec((1, 1, heads, DK, DV), per_chunk),
            pl.BlockSpec((1, rows, heads * DV), per_row),
        ],
        out_shape=[
            jax.ShapeDtypeStruct((seqs, tokens, heads * DV), BF16),
            jax.ShapeDtypeStruct((seqs, chunks, heads, rows, rows), BF16),
            jax.ShapeDtypeStruct((seqs, tokens, heads * DV), BF16),
            jax.ShapeDtypeStruct((seqs, chunks, heads, DK, DV), F32),
            jax.ShapeDtypeStruct((seqs, tokens, heads * DV), F32),
        ],
        scratch_shapes=[pltpu.VMEM((heads, DK, DV), F32)],
        compiler_params=pltpu.CompilerParams(vmem_limit_bytes=48 * 1024 * 1024),
        cost_estimate=pl.CostEstimate(
            flops=seqs * chunks * heads * 30 * 2 * rows**3,
            bytes_accessed=12 * 1024 * 1024,
            transcendentals=seqs * tokens * width,
        ),
        name="mixer_forward",
    )(projected, projected, filters, side, gain)


def mixer_backward(projected, filters, side, gain, adjoint, saved, heads):
    seqs, tokens, width, rows, chunks, conv_width = mixer_sizes(projected, heads)
    ratio = rows // 16
    solved, update, start, raw = saved
    per_row = lambda s, c: (s, chunks - 1 - c, 0)
    fixed = lambda s, c: (0, 0)
    per_chunk = lambda s, c: (s, chunks - 1 - c, 0, 0, 0)
    return pl.pallas_call(
        functools.partial(mixer_backward_kernel, heads=heads, chunks=chunks),
        grid=(seqs, chunks),
        in_specs=[
            pl.BlockSpec((1, rows, width), per_row),
            pl.BlockSpec(
                (1, 16, width),
                lambda s, c: (s, jnp.maximum((chunks - 1 - c) * ratio - 1, 0), 0),
            ),
            pl.BlockSpec((4, conv_width), fixed),
            pl.BlockSpec((8, LANES), fixed),
            pl.BlockSpec((1, DV), fixed),
            pl.BlockSpec((1, rows, heads * DV), per_row),
            pl.BlockSpec((1, 1, heads, rows, rows), per_chunk),
            pl.BlockSpec((1, rows, heads * DV), per_row),
            pl.BlockSpec((1, 1, heads, DK, DV), per_chunk),
            pl.BlockSpec((1, rows, heads * DV), per_row),
        ],
        out_specs=[
            pl.BlockSpec((1, rows, width), per_row),
            pl.BlockSpec((4, conv_width), fixed),
            pl.BlockSpec((8, LANES), fixed),
            pl.BlockSpec((1, DV), fixed),
        ],
        out_shape=[
            jax.ShapeDtypeStruct((seqs, tokens, width), BF16),
            jax.ShapeDtypeStruct((4, conv_width), F32),
            jax.ShapeDtypeStruct((8, LANES), F32),
            jax.ShapeDtypeStruct((1, DV), F32),
        ],
        scratch_shapes=[
            pltpu.VMEM((heads, DK, DV), F32),
            pltpu.VMEM((8, conv_width), F32),
        ],
        compiler_params=pltpu.CompilerParams(vmem_limit_bytes=48 * 1024 * 1024),
        cost_estimate=pl.CostEstimate(
            flops=seqs * chunks * heads * 40 * 2 * rows**3,
            bytes_accessed=16 * 1024 * 1024,
            transcendentals=seqs * tokens * width,
        ),
        name="mixer_backward",
    )(projected, projected, filters, side, gain, adjoint, solved, update, start, raw)


def shift_pairs(count, by):
    return [(place, (place + by) % count) for place in range(count)]


def swap_pairs(count, mask):
    return [(place, place ^ mask) for place in range(count)]


def put_block(whole, block, place):
    return lax.dynamic_update_slice(whole, block[None], (place,) + (0,) * block.ndim)


def ring_gather(block, axis):
    count = lax.axis_size(axis)
    me = lax.axis_index(axis)
    whole = put_block(jnp.zeros((count,) + block.shape, block.dtype), block, me)
    right, left = block, block
    far = count // 2 if count % 2 == 0 else 0
    for hop in range(1, (count - 1) // 2 + 1):
        right = lax.ppermute(right, axis, shift_pairs(count, 1))
        left = lax.ppermute(left, axis, shift_pairs(count, -1))
        whole = put_block(whole, right, (me - hop) % count)
        whole = put_block(whole, left, (me + hop) % count)
    if far:
        half = block.shape[0] // 2
        right = lax.ppermute(right[:half], axis, shift_pairs(count, 1))
        left = lax.ppermute(left[half:], axis, shift_pairs(count, -1))
        whole = put_block(whole, right, (me + far) % count)
        whole = lax.dynamic_update_slice(
            whole, left[None], ((me + far) % count, half) + (0,) * (block.ndim - 1)
        )
    return whole


def take_block(whole, place):
    return lax.dynamic_index_in_dim(whole, place, 0, keepdims=False)


def ring_reduce(whole, axis):
    count = lax.axis_size(axis)
    me = lax.axis_index(axis)
    total = take_block(whole, me)
    if count == 1:
        return total
    half = total.shape[0] // 2
    reach = (count - 1) // 2
    right = left = None
    if count % 2 == 0:
        far = take_block(whole, (me + count // 2) % count)
        right = lax.ppermute(far[:half].astype(BF16), axis, shift_pairs(count, 1)).astype(F32)
        left = lax.ppermute(far[half:].astype(BF16), axis, shift_pairs(count, -1)).astype(F32)
    for hop in range(reach, 0, -1):
        ahead = take_block(whole, (me + hop) % count)
        behind = take_block(whole, (me - hop) % count)
        if right is not None and right.shape[0] == half:
            ahead = jnp.concatenate([ahead[:half] + right, ahead[half:]], axis=0)
            behind = jnp.concatenate([behind[:half], behind[half:] + left], axis=0)
        elif right is not None:
            ahead, behind = ahead + right, behind + left
        right = lax.ppermute(ahead.astype(BF16), axis, shift_pairs(count, 1)).astype(F32)
        left = lax.ppermute(behind.astype(BF16), axis, shift_pairs(count, -1)).astype(F32)
    if right.shape[0] == half:
        return total + jnp.concatenate([right, left], axis=0)
    return total + right + left


def exchange(whole, axis):
    count = lax.axis_size(axis)
    me = lax.axis_index(axis)
    result = put_block(jnp.zeros(whole.shape, whole.dtype), take_block(whole, me), me)
    for hop in range(1, count):
        moved = lax.ppermute(
            take_block(whole, (me + hop) % count), axis, shift_pairs(count, hop)
        )
        result = put_block(result, moved, (me - hop) % count)
    return result


def plane_gather(block):
    count = lax.axis_size("dp")
    if count != 8:
        return lax.all_gather(block, "dp", axis=0, tiled=False)
    me = lax.axis_index("dp")
    half = block.shape[0] // 2
    swap = lambda part, mask: lax.ppermute(part, "dp", swap_pairs(8, mask))
    near_two, near_four = swap(block, 2), swap(block, 4)
    far = jnp.concatenate([swap(near_two[:half], 4), swap(near_four[half:], 2)], axis=0)
    whole = jnp.zeros((8,) + block.shape, block.dtype)
    for mask, part in ((0, block), (2, near_two), (4, near_four), (6, far)):
        whole = put_block(whole, part, me ^ mask)
        whole = put_block(whole, swap(part, 1), me ^ mask ^ 1)
    return whole


def plane_reduce(whole):
    count = lax.axis_size("dp")
    if count != 8:
        return lax.psum_scatter(
            whole.astype(BF16), "dp", scatter_dimension=0, tiled=False
        ).astype(F32)
    me = lax.axis_index("dp")
    half = whole.shape[1] // 2
    swap = lambda part, mask: lax.ppermute(part.astype(BF16), "dp", swap_pairs(8, mask)).astype(
        F32
    )
    lane = {
        mask: take_block(whole, me ^ mask) + swap(take_block(whole, me ^ mask ^ 1), 1)
        for mask in (6, 2, 4, 0)
    }
    via_four = swap(lane[6][:half], 4)
    via_two = swap(lane[6][half:], 2)
    to_two = jnp.concatenate([lane[2][:half] + via_four, lane[2][half:]], axis=0)
    to_four = jnp.concatenate([lane[4][:half], lane[4][half:] + via_two], axis=0)
    return lane[0] + swap(to_two, 2) + swap(to_four, 4)


def sum_everywhere(values):
    for axis in ("dp", "seq"):
        count = lax.axis_size(axis)
        if count & (count - 1):
            values = lax.psum(values, axis)
            continue
        mask = 1
        while mask < count:
            values = values + lax.ppermute(values, axis, swap_pairs(count, mask))
            mask *= 2
    return values


def round_up(size, step):
    return (size + step - 1) // step * step


def rms_parts(values):
    scale = lax.rsqrt(jnp.mean(values * values, axis=-1, keepdims=True) + 1e-05)
    return values * scale, scale


def rms_back(unit, scale, gain, adjoint):
    scaled = adjoint * gain
    return scale * (scaled - unit * jnp.mean(scaled * unit, axis=-1, keepdims=True))


def dot(left, right):
    return jnp.dot(left, right, preferred_element_type=F32)


def dot_nt(left, right):
    return jnp.einsum("tc,dc->td", left, right, preferred_element_type=F32)


def dot_tn(left, right):
    return jnp.einsum("tr,tc->rc", left, right, preferred_element_type=F32)


def by_heads(weight, ns):
    return jnp.swapaxes(weight.reshape(weight.shape[0], ns, weight.shape[1] // ns), 0, 1)


def pad_last(values, size):
    if values.shape[-1] == size:
        return values
    return jnp.pad(values, [(0, 0)] * (values.ndim - 1) + [(0, size - values.shape[-1])])


def hidden_out(weight, nd, ns, padded):
    rows, hidden = weight.shape
    block = hidden // (nd * ns)
    parts = jnp.transpose(weight.reshape(rows, nd, ns, block), (2, 0, 1, 3))
    return pad_last(parts.reshape(ns, rows, nd * block), padded)


def hidden_back(parts, nd, hidden):
    ns, rows, _ = parts.shape
    block = hidden // (nd * ns)
    kept = parts[:, :, : nd * block].reshape(ns, rows, nd, block)
    return jnp.transpose(kept, (1, 2, 0, 3)).reshape(rows, hidden)


def shards(
    inputs,
    cotangent,
    query_proj,
    key_proj,
    value_proj,
    gate_proj,
    rate_proj,
    output_proj,
    ffn_gate,
    ffn_up,
    ffn_down,
    mixer_gain,
    ffn_gain,
    query_filter,
    key_filter,
    value_filter,
    decay_log,
    step_bias,
    head_gain,
):
    seqs, piece, width = inputs.shape
    ns, nd = lax.axis_size("seq"), lax.axis_size("dp")
    me = lax.axis_index("seq")
    heads = H // ns
    kq, kv = heads * DK, heads * DV
    own = seqs * piece
    tokens = own * ns
    rows = query_proj.shape[0]
    hidden = ffn_gate.shape[1]
    hidden_own = hidden // ns
    padded = round_up(hidden_own, LANES)

    def to_pieces(values):
        cut = values.reshape((seqs, ns, piece) + values.shape[1:])
        return jnp.swapaxes(cut, 0, 1).reshape((ns, own) + values.shape[1:])

    def from_pieces(values):
        cut = values.reshape((ns, seqs, piece) + values.shape[2:])
        return jnp.swapaxes(cut, 0, 1).reshape((tokens,) + values.shape[2:])

    flat_in = inputs.reshape(own, width)
    flat_cot = cotangent.reshape(own, width)
    mixer_local = jnp.concatenate(
        [by_heads(w, ns) for w in (query_proj, key_proj, value_proj, gate_proj)]
        + [pad_last(by_heads(rate_proj, ns), LANES)],
        axis=2,
    )
    mixer_rows = exchange(mixer_local, "seq").reshape(ns * rows, mixer_local.shape[2])
    mixer_weight = plane_gather(mixer_rows).reshape(width, mixer_local.shape[2])
    all_in = from_pieces(ring_gather(flat_in, "seq"))
    out_rows = ring_gather(output_proj, "seq").reshape(ns * output_proj.shape[0], width)
    out_weight = plane_gather(out_rows).reshape(H * DV, width)
    ffn_local = jnp.concatenate(
        [hidden_out(ffn_gate, nd, ns, padded), hidden_out(ffn_up, nd, ns, padded)], axis=2
    )
    ffn_rows = exchange(ffn_local, "seq").reshape(ns * rows, 2 * padded)
    ffn_weight = plane_gather(ffn_rows).reshape(width, 2 * padded)
    down_weight = plane_gather(ffn_down).reshape(hidden_own, width)
    down_weight = jnp.pad(down_weight, ((0, padded - hidden_own), (0, 0)))
    all_cot = from_pieces(ring_gather(flat_cot, "seq"))

    unit_in, scale_in = rms_parts(all_in.astype(F32))
    normed = (unit_in * mixer_gain).astype(BF16)
    projected = dot(normed, mixer_weight).astype(BF16).reshape(seqs, ns * piece, -1)
    own_cols = lambda table, size: lax.dynamic_slice_in_dim(table, me * size, size, 1)
    filters = jnp.concatenate(
        [own_cols(query_filter, kq), own_cols(key_filter, kq), own_cols(value_filter, kv)], axis=1
    )
    own_decay = jnp.exp(lax.dynamic_slice_in_dim(decay_log, me * heads, heads, 0))
    own_bias = lax.dynamic_slice_in_dim(step_bias, me * heads, heads, 0)
    spread = lambda values: pad_last(
        jnp.stack([jnp.zeros_like(values), values], axis=1).reshape(1, 2 * heads), LANES
    )
    side = jnp.concatenate(
        [spread(own_decay), spread(own_bias), jnp.zeros((6, LANES), F32)], axis=0
    )
    gain_row = head_gain.reshape(1, DV)
    mixed, *saved = mixer_forward(projected, filters, side, gain_row, heads)
    mixed_pieces = exchange(to_pieces(mixed.reshape(tokens, kv)), "seq")
    mixed_low = jnp.swapaxes(mixed_pieces, 0, 1).reshape(own, H * DV)

    middle = flat_in.astype(F32) + dot(mixed_low, out_weight)
    unit_two, scale_two = rms_parts(middle)
    second_all = from_pieces(ring_gather((unit_two * ffn_gain).astype(BF16), "seq"))
    hidden_both = dot(second_all, ffn_weight)
    hidden_gate, hidden_up = hidden_both[:, :padded], hidden_both[:, padded:]
    gate_sig = jax.nn.sigmoid(hidden_gate)
    gate_silu = hidden_gate * gate_sig
    active = (gate_silu * hidden_up).astype(BF16)
    block_sum = ring_reduce(to_pieces(dot(active, down_weight)), "seq")
    block_out = (middle + block_sum).astype(BF16).reshape(inputs.shape)

    adj_act = dot_nt(all_cot, down_weight)
    adj_gate = adj_act * hidden_up * silu_slope(hidden_gate, gate_sig)
    adj_both = jnp.concatenate(
        [adj_gate.astype(BF16), (adj_act * gate_silu).astype(BF16)], axis=1
    )
    adj_second = ring_reduce(to_pieces(dot_nt(adj_both, ffn_weight)), "seq")
    grad_down = dot_tn(active, all_cot)[:hidden_own].reshape(nd, -1, width)
    grad_ffn = dot_tn(second_all, adj_both).reshape(nd, ns * rows, 2 * padded)
    down_out = plane_reduce(grad_down).astype(BF16)
    ffn_parts = exchange(plane_reduce(grad_ffn).astype(BF16).reshape(ns, rows, -1), "seq")
    ffngate_out = hidden_back(ffn_parts[:, :, :padded], nd, hidden)
    ffnup_out = hidden_back(ffn_parts[:, :, padded:], nd, hidden)

    gain_two = jnp.sum(adj_second * unit_two, axis=0)
    adj_middle = flat_cot.astype(F32) + rms_back(unit_two, scale_two, ffn_gain, adj_second)
    attn_low = adj_middle.astype(BF16)
    adj_mixed = dot_nt(attn_low, out_weight).astype(BF16)
    adj_heads = from_pieces(
        exchange(jnp.swapaxes(adj_mixed.reshape(own, ns, kv), 0, 1), "seq")
    ).reshape(seqs, ns * piece, kv)
    grad_out = dot_tn(mixed_low, attn_low).reshape(nd, -1, width)
    grad_out = plane_reduce(grad_out)
    out_out = ring_reduce(grad_out.reshape(ns, -1, width), "seq").astype(BF16)

    adj_projected, filter_sum, side_sum, gain_sum = mixer_backward(
        projected, filters, side, gain_row, adj_heads, saved, heads
    )
    adj_projected = adj_projected.reshape(tokens, -1)
    adj_partial = dot_nt(adj_projected, mixer_weight)
    gain_one = jnp.sum(adj_partial * unit_in, axis=0)
    adj_normed = ring_reduce(to_pieces(adj_partial), "seq")
    grad_mixer = dot_tn(normed, adj_projected).reshape(nd, ns * rows, -1)
    mixer_parts = exchange(plane_reduce(grad_mixer).astype(BF16).reshape(ns, rows, -1), "seq")
    whole_rows = lambda parts: jnp.swapaxes(parts, 0, 1).reshape(rows, -1)
    query_out = whole_rows(mixer_parts[:, :, :kq])
    key_out = whole_rows(mixer_parts[:, :, kq : 2 * kq])
    value_out = whole_rows(mixer_parts[:, :, 2 * kq : 2 * kq + kv])
    gate_out = whole_rows(mixer_parts[:, :, 2 * kq + kv : 2 * kq + 2 * kv])
    rate_at = 2 * kq + 2 * kv
    rate_out = whole_rows(mixer_parts[:, :, rate_at : rate_at + 2 * heads])

    unit_one, scale_one = rms_parts(flat_in.astype(F32))
    grad_inputs = (
        (adj_middle + rms_back(unit_one, scale_one, mixer_gain, adj_normed))
        .astype(BF16)
        .reshape(inputs.shape)
    )

    def place(own_part, table, size):
        return lax.dynamic_update_slice_in_dim(
            jnp.zeros(table.shape, F32), own_part, me * size, table.ndim - 1
        )

    small = (
        gain_one,
        gain_two,
        place(filter_sum[:, :kq], query_filter, kq),
        place(filter_sum[:, kq : 2 * kq], key_filter, kq),
        place(filter_sum[:, 2 * kq :], value_filter, kv),
        place(side_sum[0, 1 : 2 * heads : 2], decay_log, heads),
        place(side_sum[1, 1 : 2 * heads : 2], step_bias, heads),
        gain_sum.reshape(DV),
    )
    packed = jnp.concatenate([pad_last(part.reshape(-1), round_up(part.size, LANES)) for part in small])
    packed = sum_everywhere(packed.reshape(-1, LANES)).astype(BF16).reshape(-1)
    outs = []
    at = 0
    for part in small:
        outs.append(packed[at : at + part.size].reshape(part.shape))
        at += round_up(part.size, LANES)
    return (
        block_out,
        grad_inputs,
        query_out,
        key_out,
        value_out,
        gate_out,
        rate_out,
        out_out,
        ffngate_out,
        ffnup_out,
        down_out,
        *outs,
    )


def solution(mesh):
    tokens = P("dp", "seq", None)
    weight = P(("dp", "seq"), None)
    specs = (tokens,) * 2 + (weight,) * 9 + (P(),) * 8
    return jax.shard_map(shards, mesh=mesh, in_specs=specs, out_specs=specs, check_vma=False)
```

```python
import functools

import jax
import jax.numpy as jnp
from jax import lax
from jax.experimental import pallas as pl
from jax.experimental.pallas import tpu as pltpu
from jax.sharding import PartitionSpec as P

H = 8
DK = 128
DV = 256


CHUNK = 256
LANES = 128
F32 = jnp.float32
BF16 = jnp.bfloat16


def mm(left, right, left_dim=1, right_dim=0):
    return lax.dot_general(
        left.astype(BF16),
        right.astype(BF16),
        (((left_dim,), (right_dim,)), ((), ())),
        preferred_element_type=F32,
    )


def mm_nt(left, right):
    return mm(left, right, 1, 1)


def mm_tn(left, right):
    return mm(left, right, 0, 0)


def iota(shape, axis):
    return lax.broadcasted_iota(jnp.int32, shape, axis)


def exact_mm(ones, values):
    first = values.astype(BF16)
    rest = values - first.astype(F32)
    second = rest.astype(BF16)
    third = (rest - second.astype(F32)).astype(BF16)
    return mm(ones, first) + mm(ones, second) + mm(ones, third)


def small_inverse(coupling):
    size = coupling.shape[0]
    rows = iota(coupling.shape, 0)
    cols = iota(coupling.shape, 1)
    solved = jnp.where((rows // 2 == cols // 2), -coupling, 0.0)
    width = 2
    while width < size:
        band = (rows // (2 * width) == cols // (2 * width)) & (rows // width != cols // width)
        part = jnp.where(band, coupling, 0.0)
        step = part + mm(part, solved)
        solved = solved - step - mm(solved, step)
        width = 2 * width
    return solved


def lower_inverse(coupling):
    size = coupling.shape[0]
    if size <= LANES:
        return small_inverse(coupling)
    half = size // 2
    head = lower_inverse(coupling[:half, :half])
    tail = lower_inverse(coupling[half:, half:])
    part = coupling[half:, :half]
    step = part + mm(part, head)
    corner = -step - mm(tail, step)
    top = jnp.concatenate([head, jnp.zeros((half, half), F32)], axis=1)
    return jnp.concatenate([top, jnp.concatenate([corner, tail], axis=1)], axis=0)


def silu_slope(values, gate):
    return gate * (1.0 + values * (1.0 - gate))


def softplus(values):
    return jnp.maximum(values, 0.0) + jnp.log1p(jnp.exp(-jnp.abs(values)))


def conv_taps(current, before, first_chunk):
    before = jnp.where(first_chunk, 0.0, before.astype(F32))
    joined = jnp.concatenate([before, current.astype(F32)], axis=0)
    top = before.shape[0]
    rows = current.shape[0]
    return [joined[top - 3 + tap : top - 3 + tap + rows] for tap in range(4)]


def decay_parts(rate, decay_scale, decay_bias):
    rows = rate.shape[0]
    shifted = rate + decay_bias
    log_decay = -decay_scale * softplus(shifted)
    lower = jnp.where(iota((rows, rows), 0) >= iota((rows, rows), 1), 1.0, 0.0)
    running = exact_mm(lower, log_decay)
    return shifted, log_decay, running


def head_parts(summed, running, running_rows, head, heads):
    rows = summed.shape[0]
    gates = jax.nn.sigmoid(summed)
    conv = summed * gates
    q_at, k_at, v_at = head * DK, (heads + head) * DK, 2 * heads * DK + head * DV
    q_conv, k_conv = conv[:, q_at : q_at + DK], conv[:, k_at : k_at + DK]
    value = conv[:, v_at : v_at + DV]
    q_scale = lax.rsqrt(jnp.sum(q_conv * q_conv, axis=1, keepdims=True) + 1e-06)
    k_scale = lax.rsqrt(jnp.sum(k_conv * k_conv, axis=1, keepdims=True) + 1e-06)
    query = q_conv * (q_scale * DK**-0.5)
    key = k_conv * k_scale
    lane = 2 * head + 1
    total = running[:, lane : lane + 1]
    across = running_rows[lane : lane + 1, :]
    lower = iota((rows, rows), 0) >= iota((rows, rows), 1)
    decays = jnp.where(lower, jnp.exp(jnp.minimum(total - across, 0.0)), 0.0)
    last = total[rows - 1 : rows, :]
    return q_conv, k_conv, q_scale, k_scale, query, key, value, total, decays, last


def mixer_forward_kernel(
    order_ref, current_ref, before_ref, filter_ref, side_ref, gain_ref,
    mixed_ref, solved_ref, update_ref, start_ref, raw_ref, memory_ref, *, heads
):
    chunk = pl.program_id(1)

    @pl.when(chunk == 0)
    def _():
        memory_ref[...] = jnp.zeros(memory_ref.shape, F32)

    conv_width = 2 * heads * DK + heads * DV
    gate_at = conv_width
    rate_at = conv_width + heads * DV
    taps = conv_taps(
        current_ref[:, :conv_width], before_ref[:, :conv_width], chunk == 0
    )
    rows = taps[0].shape[0]
    summed = taps[0] * filter_ref[0:1, :]
    for tap in range(1, 4):
        summed = summed + taps[tap] * filter_ref[tap : tap + 1, :]
    rate = current_ref[:, rate_at : rate_at + LANES].astype(F32)
    strengths = jax.nn.sigmoid(rate)
    shifted, log_decay, running = decay_parts(rate, side_ref[0:1, :], side_ref[1:2, :])
    running_rows = running.T
    strict = iota((rows, rows), 0) > iota((rows, rows), 1)
    for head in range(heads):
        _, _, _, _, query, key, value, total, decays, last = head_parts(
            summed, running, running_rows, head, heads
        )
        strength = strengths[:, 2 * head : 2 * head + 1]
        scaling = jnp.exp(total)
        inner = mm_nt(key, key)
        coupling = jnp.where(strict, strength * inner * decays, 0.0)
        solved = lower_inverse(coupling)
        start = memory_ref[head]
        target = strength * (value - scaling * mm(key, start))
        update = target + mm(solved, target)
        scores = mm_nt(query, key) * decays
        raw = scaling * mm(query, start) + mm(scores, update)
        tail = key * jnp.exp(last - total)
        memory_ref[head] = jnp.exp(last) * start + mm_tn(tail, update)
        start_ref[0, 0, head] = start
        solved_ref[0, 0, head] = solved.astype(BF16)
        at = head * DV
        update_ref[:, at : at + DV] = update.astype(BF16)
        raw_ref[:, at : at + DV] = raw
        gate = current_ref[:, gate_at + at : gate_at + at + DV].astype(F32)
        normal = raw * lax.rsqrt(jnp.mean(raw * raw, axis=1, keepdims=True) + 1e-05)
        mixed_ref[:, at : at + DV] = (
            normal * gain_ref[...] * (gate * jax.nn.sigmoid(gate))
        ).astype(BF16)


def mixer_backward_kernel(
    order_ref, current_ref, before_ref, filter_ref, side_ref, gain_ref,
    adjoint_ref, solved_ref, update_ref, start_ref, raw_ref,
    grad_ref, filter_sum_ref, side_sum_ref, gain_sum_ref, memory_ref, after_ref, *, heads, chunks
):
    step = pl.program_id(1)

    @pl.when(step == 0)
    def _():
        memory_ref[...] = jnp.zeros(memory_ref.shape, F32)
        after_ref[...] = jnp.zeros(after_ref.shape, F32)

    @pl.when((step == 0) & (pl.program_id(0) == 0))
    def _():
        filter_sum_ref[...] = jnp.zeros(filter_sum_ref.shape, F32)
        side_sum_ref[...] = jnp.zeros(side_sum_ref.shape, F32)
        gain_sum_ref[...] = jnp.zeros(gain_sum_ref.shape, F32)

    conv_width = 2 * heads * DK + heads * DV
    gate_at = conv_width
    rate_at = conv_width + heads * DV
    taps = conv_taps(
        current_ref[:, :conv_width], before_ref[:, :conv_width], step == chunks - 1
    )
    rows = taps[0].shape[0]
    summed = taps[0] * filter_ref[0:1, :]
    for tap in range(1, 4):
        summed = summed + taps[tap] * filter_ref[tap : tap + 1, :]
    rate = current_ref[:, rate_at : rate_at + LANES].astype(F32)
    strengths = jax.nn.sigmoid(rate)
    decay_scale = side_ref[0:1, :]
    shifted, log_decay, running = decay_parts(rate, decay_scale, side_ref[1:2, :])
    running_rows = running.T
    strict = iota((rows, rows), 0) > iota((rows, rows), 1)
    lane_ids = iota((rows, LANES), 1)
    row_ids = iota((LANES, rows), 0)
    last_lanes = iota((1, LANES), 1)
    sum_across = jnp.zeros((rows, LANES), F32)
    sum_down = jnp.zeros((LANES, rows), F32)
    sum_last = jnp.zeros((1, LANES), F32)
    adj_strength = jnp.zeros((rows, LANES), F32)
    q_adjoints, k_adjoints, v_adjoints = [], [], []
    for head in range(heads):
        q_conv, k_conv, q_scale, k_scale, query, key, value, total, decays, last = head_parts(
            summed, running, running_rows, head, heads
        )
        strength = strengths[:, 2 * head : 2 * head + 1]
        scaling = jnp.exp(total)
        at = head * DV
        raw = raw_ref[:, at : at + DV]
        gate = current_ref[:, gate_at + at : gate_at + at + DV].astype(F32)
        gate_sig = jax.nn.sigmoid(gate)
        gate_silu = gate * gate_sig
        adj_mixed = adjoint_ref[:, at : at + DV].astype(F32)
        inv = lax.rsqrt(jnp.mean(raw * raw, axis=1, keepdims=True) + 1e-05)
        normal = raw * inv
        upstream = adj_mixed * gain_ref[...] * gate_silu
        adj_raw = inv * (
            upstream - normal * jnp.mean(upstream * normal, axis=1, keepdims=True)
        )
        adj_gate = adj_mixed * normal * gain_ref[...] * silu_slope(gate, gate_sig)
        grad_ref[:, gate_at + at : gate_at + at + DV] = adj_gate.astype(BF16)
        gain_sum_ref[...] += jnp.sum(adj_mixed * normal * gate_silu, axis=0, keepdims=True)

        start = start_ref[0, 0, head]
        solved = solved_ref[0, 0, head]
        update = update_ref[:, at : at + DV]
        adj_memory = memory_ref[head]
        tail_decay = jnp.exp(last - total)
        last_decay = jnp.exp(last)
        inner = mm_nt(key, key)
        scores = mm_nt(query, key) * decays
        spread = mm(key * tail_decay, adj_memory)
        adj_update = mm_tn(scores, adj_raw) + spread
        adj_target = adj_update + mm_tn(solved, adj_update)
        adj_scores = mm_nt(adj_raw, update)
        adj_coupling = jnp.where(strict, -mm_nt(adj_target, update), 0.0) * decays
        adj_inner = strength * adj_coupling
        from_inner = adj_coupling * inner
        adj_qk = adj_scores * decays
        key_start = mm(key, start)
        query_start = mm(query, start)
        adj_query = scaling * mm_nt(adj_raw, start) + mm(adj_qk, key)
        adj_key = (
            mm_tn(adj_qk, query)
            + tail_decay * mm_nt(update, adj_memory)
            - scaling * strength * mm_nt(adj_target, start)
            + mm(adj_inner, key)
            + mm_tn(adj_inner, key)
        )
        adj_value = strength * adj_target
        strength_sum = jnp.sum(
            adj_target * (value - scaling * key_start), axis=1, keepdims=True
        ) + jnp.sum(from_inner, axis=1, keepdims=True)
        pairs = adj_scores * scores + strength * from_inner
        tail_sum = jnp.sum(spread * update.astype(F32), axis=1, keepdims=True)
        decay_sum = (
            jnp.sum(pairs, axis=1, keepdims=True)
            + scaling * jnp.sum(query_start * adj_raw, axis=1, keepdims=True)
            - scaling * strength * jnp.sum(key_start * adj_target, axis=1, keepdims=True)
            - tail_sum
        )
        at_end = jnp.sum(tail_sum, axis=0, keepdims=True) + last_decay * jnp.sum(
            jnp.sum(start * adj_memory, axis=1, keepdims=True), axis=0, keepdims=True
        )
        lane = 2 * head + 1
        sum_across = sum_across + jnp.where(lane_ids == lane, decay_sum, 0.0)
        sum_down = sum_down + jnp.where(
            row_ids == lane, jnp.sum(pairs, axis=0, keepdims=True), 0.0
        )
        sum_last = sum_last + jnp.where(last_lanes == lane, at_end, 0.0)
        adj_strength = adj_strength + jnp.where(lane_ids == lane - 1, strength_sum, 0.0)
        memory_ref[head] = (
            last_decay * adj_memory
            + mm_tn(query * scaling, adj_raw)
            - mm_tn(key * (scaling * strength), adj_target)
        )
        adj_query = adj_query * DK**-0.5
        q_adjoints.append(
            q_scale * adj_query
            - q_conv
            * (q_scale * q_scale * q_scale * jnp.sum(q_conv * adj_query, axis=1, keepdims=True))
        )
        k_adjoints.append(
            k_scale * adj_key
            - k_conv
            * (k_scale * k_scale * k_scale * jnp.sum(k_conv * adj_key, axis=1, keepdims=True))
        )
        v_adjoints.append(adj_value)

    upper = jnp.where(iota((rows, rows), 0) <= iota((rows, rows), 1), 1.0, 0.0)
    adj_log_decay = exact_mm(upper, sum_across - sum_down.T) + sum_last
    adj_shifted = -adj_log_decay * decay_scale * jax.nn.sigmoid(shifted)
    adj_rate = adj_shifted + adj_strength * strengths * (1.0 - strengths)
    grad_ref[:, rate_at : rate_at + LANES] = adj_rate.astype(BF16)
    side_sum_ref[0:1, :] += jnp.sum(adj_log_decay * log_decay, axis=0, keepdims=True)
    side_sum_ref[1:2, :] += jnp.sum(adj_shifted, axis=0, keepdims=True)

    adj_conv = jnp.concatenate(q_adjoints + k_adjoints + v_adjoints, axis=1)
    adj_summed = adj_conv * silu_slope(summed, jax.nn.sigmoid(summed))
    joined = jnp.concatenate([adj_summed, after_ref[...]], axis=0)
    after_ref[...] = adj_summed[0:8]
    adj_pre = adj_summed * filter_ref[3:4, :]
    filter_sum_ref[3:4, :] += jnp.sum(adj_summed * taps[3], axis=0, keepdims=True)
    for tap in range(3):
        adj_pre = adj_pre + joined[3 - tap : 3 - tap + rows] * filter_ref[tap : tap + 1, :]
        filter_sum_ref[tap : tap + 1, :] += jnp.sum(adj_summed * taps[tap], axis=0, keepdims=True)
    grad_ref[:, :conv_width] = adj_pre.astype(BF16)


def mixer_call(kernel, order, heads, rows, seqs, chunks, backward, operands, outs, scratch, name):
    ratio = rows // 16
    natural = lambda c: chunks - 1 - c if backward else c
    block = lambda s, c, order_ref: order_ref[s * chunks + natural(c)]

    def before(s, c, order_ref):
        previous = order_ref[s * chunks + jnp.maximum(natural(c) - 1, 0)]
        return (previous * ratio + ratio - 1, 0)

    def spec(array):
        if array.ndim == 5:
            return pl.BlockSpec(
                (1, 1) + array.shape[2:], lambda s, c, order_ref: (s, natural(c), 0, 0, 0)
            )
        if array.shape[0] == rows * seqs * chunks:
            return pl.BlockSpec(
                (rows, array.shape[1]), lambda s, c, order_ref: (block(s, c, order_ref), 0)
            )
        return pl.BlockSpec(array.shape, lambda s, c, order_ref: (0, 0))

    in_specs = [spec(operand) for operand in operands]
    in_specs.insert(1, pl.BlockSpec((16, operands[0].shape[1]), before))
    return pl.pallas_call(
        kernel,
        grid_spec=pltpu.PrefetchScalarGridSpec(
            num_scalar_prefetch=1,
            grid=(seqs, chunks),
            in_specs=in_specs,
            out_specs=[spec(out) for out in outs],
            scratch_shapes=scratch,
        ),
        out_shape=outs,
        compiler_params=pltpu.CompilerParams(vmem_limit_bytes=48 * 1024 * 1024),
        cost_estimate=pl.CostEstimate(
            flops=seqs * chunks * heads * 60 * 2 * rows**3,
            bytes_accessed=24 * 1024 * 1024,
            transcendentals=rows * seqs * chunks * 1024,
        ),
        name=name,
    )(order, operands[0], *operands)


def mixer_forward(projected, filters, side, gain, order, heads, seqs, rows):
    tokens = projected.shape[0]
    chunks = tokens // (rows * seqs)
    shape = jax.ShapeDtypeStruct
    return mixer_call(
        functools.partial(mixer_forward_kernel, heads=heads),
        order, heads, rows, seqs, chunks, False,
        (projected, filters, side, gain),
        [
            shape((tokens, heads * DV), BF16),
            shape((seqs, chunks, heads, rows, rows), BF16),
            shape((tokens, heads * DV), BF16),
            shape((seqs, chunks, heads, DK, DV), F32),
            shape((tokens, heads * DV), F32),
        ],
        [pltpu.VMEM((heads, DK, DV), F32)],
        "mixer_forward",
    )


def mixer_backward(projected, filters, side, gain, adjoint, saved, order, heads, seqs, rows):
    tokens = projected.shape[0]
    chunks = tokens // (rows * seqs)
    shape = jax.ShapeDtypeStruct
    return mixer_call(
        functools.partial(mixer_backward_kernel, heads=heads, chunks=chunks),
        order, heads, rows, seqs, chunks, True,
        (projected, filters, side, gain, adjoint, *saved),
        [
            shape(projected.shape, BF16),
            shape(filters.shape, F32),
            shape((8, LANES), F32),
            shape((1, DV), F32),
        ],
        [pltpu.VMEM((heads, DK, DV), F32), pltpu.VMEM((8, filters.shape[1]), F32)],
        "mixer_backward",
    )


def shift_pairs(count, by):
    return [(place, (place + by) % count) for place in range(count)]


def swap_pairs(count, mask):
    return [(place, place ^ mask) for place in range(count)]


def put_block(whole, block, place):
    return lax.dynamic_update_slice(whole, block[None], (place,) + (0,) * block.ndim)


def ring_gather(block, axis):
    count = lax.axis_size(axis)
    found = {0: block}
    right, left = block, block
    for hop in range(1, (count - 1) // 2 + 1):
        right = lax.ppermute(right, axis, shift_pairs(count, 1))
        left = lax.ppermute(left, axis, shift_pairs(count, -1))
        found[count - hop] = right
        found[hop] = left
    if count % 2 == 0:
        half = block.shape[0] // 2
        right = lax.ppermute(right[:half], axis, shift_pairs(count, 1))
        left = lax.ppermute(left[half:], axis, shift_pairs(count, -1))
        found[count // 2] = jnp.concatenate([right, left], axis=0)
    return jnp.concatenate([found[hop] for hop in range(count)], axis=0)


def take_block(whole, place):
    return lax.dynamic_index_in_dim(whole, place, 0, keepdims=False)


def ring_reduce(whole, axis):
    count = lax.axis_size(axis)
    blocks = whole.reshape((count, whole.shape[0] // count) + whole.shape[1:])
    total = blocks[0]
    if count == 1:
        return total, total
    half = total.shape[0] // 2
    first = total
    move = lambda part, by: lax.ppermute(
        part.astype(BF16), axis, shift_pairs(count, by)
    ).astype(F32)
    right = left = None
    if count % 2 == 0:
        far = blocks[count // 2]
        right, left = move(far[:half], 1), move(far[half:], -1)
        first = right
    for hop in range((count - 1) // 2, 0, -1):
        ahead, behind = blocks[hop], blocks[count - hop]
        if right is not None and right.shape[0] == half:
            ahead = jnp.concatenate([ahead[:half] + right, ahead[half:]], axis=0)
            behind = jnp.concatenate([behind[:half], behind[half:] + left], axis=0)
        elif right is not None:
            ahead, behind = ahead + right, behind + left
        right, left = move(ahead, 1), move(behind, -1)
    if right.shape[0] == half:
        return total + jnp.concatenate([right, left], axis=0), first
    return total + right + left, first


def hand_out(blocks, axis, by):
    count = lax.axis_size(axis)
    return [blocks[0]] + [
        lax.ppermute(blocks[hop], axis, shift_pairs(count, hop * by)) for hop in range(1, count)
    ]


def exchange(whole, axis):
    count = lax.axis_size(axis)
    me = lax.axis_index(axis)
    result = put_block(jnp.zeros(whole.shape, whole.dtype), take_block(whole, me), me)
    for hop in range(1, count):
        moved = lax.ppermute(
            take_block(whole, (me + hop) % count), axis, shift_pairs(count, hop)
        )
        result = put_block(result, moved, (me - hop) % count)
    return result


def after(values, *others):
    return lax.optimization_barrier((values, *others))[0]


def sum_everywhere(values):
    for axis in ("dp", "seq"):
        count = lax.axis_size(axis)
        if count & (count - 1):
            values = lax.psum(values, axis)
            continue
        mask = 1
        while mask < count:
            values = values + lax.ppermute(values, axis, swap_pairs(count, mask))
            mask *= 2
    return values


def round_up(size, step):
    return (size + step - 1) // step * step


def rms_parts(values):
    scale = lax.rsqrt(jnp.mean(values * values, axis=-1, keepdims=True) + 1e-05)
    return values * scale, scale


def rms_back(unit, scale, gain, adjoint):
    scaled = adjoint * gain
    return scale * (scaled - unit * jnp.mean(scaled * unit, axis=-1, keepdims=True))


def dot(left, right):
    return jnp.dot(left, right, preferred_element_type=F32)


def dot_nt(left, right):
    return jnp.einsum("tc,dc->td", left, right, preferred_element_type=F32)


def dot_tn(left, right):
    return jnp.einsum("tr,tc->rc", left, right, preferred_element_type=F32)


def by_heads(weight, ns):
    return jnp.swapaxes(weight.reshape(weight.shape[0], ns, weight.shape[1] // ns), 0, 1)


def pad_last(values, size):
    if values.shape[-1] == size:
        return values
    return jnp.pad(values, [(0, 0)] * (values.ndim - 1) + [(0, size - values.shape[-1])])


def hidden_out(weight, nd, ns, padded):
    rows, hidden = weight.shape
    block = hidden // (nd * ns)
    parts = jnp.transpose(weight.reshape(rows, nd, ns, block), (2, 0, 1, 3))
    return pad_last(parts.reshape(ns, rows, nd * block), padded)


def hidden_back(parts, nd, hidden):
    ns, rows, _ = parts.shape
    block = hidden // (nd * ns)
    kept = parts[:, :, : nd * block].reshape(ns, rows, nd, block)
    return jnp.transpose(kept, (1, 2, 0, 3)).reshape(rows, hidden)


def shards(
    inputs,
    cotangent,
    query_proj,
    key_proj,
    value_proj,
    gate_proj,
    rate_proj,
    output_proj,
    ffn_gate,
    ffn_up,
    ffn_down,
    mixer_gain,
    ffn_gain,
    query_filter,
    key_filter,
    value_filter,
    decay_log,
    step_bias,
    head_gain,
):
    seqs, piece, width = inputs.shape
    ns, nd = lax.axis_size("seq"), lax.axis_size("dp")
    me = lax.axis_index("seq")
    heads = H // ns
    kq, kv = heads * DK, heads * DV
    own = seqs * piece
    tokens = own * ns
    rows = query_proj.shape[0]
    hidden = ffn_gate.shape[1]
    hidden_own = hidden // ns
    padded = round_up(hidden_own, LANES)

    flat_in = inputs.reshape(own, width)
    flat_cot = cotangent.reshape(own, width)
    mixer_local = jnp.concatenate(
        [by_heads(w, ns) for w in (query_proj, key_proj, value_proj, gate_proj)]
        + [pad_last(by_heads(rate_proj, ns), LANES)],
        axis=2,
    )
    all_in = ring_gather(flat_in, "seq")
    mixer_rows = exchange(mixer_local, "seq").reshape(ns * rows, mixer_local.shape[2])
    mixer_weight = lax.all_gather(mixer_rows, "dp", axis=0, tiled=True)
    ffn_local = jnp.concatenate(
        [hidden_out(ffn_gate, nd, ns, padded), hidden_out(ffn_up, nd, ns, padded)], axis=2
    )
    out_local = after(output_proj, all_in)
    out_here = jnp.zeros((ns,) + output_proj.shape, BF16)
    for hop, rows_there in enumerate(hand_out([out_local] * ns, "seq", 1)):
        out_here = put_block(out_here, rows_there, (me - hop) % ns)
    out_rows = ns * output_proj.shape[0]
    both = jnp.concatenate([out_here.reshape(out_rows, width), ffn_down], axis=0)
    both = lax.all_gather(both, "dp", axis=0, tiled=False)
    out_weight = both[:, :out_rows].reshape(ns, kv, width)
    turned = jnp.concatenate([take_block(out_weight, (me - hop) % ns) for hop in range(ns)], axis=0)
    down_weight = both[:, out_rows:].reshape(hidden_own, width)
    down_weight = jnp.pad(down_weight, ((0, padded - hidden_own), (0, 0)))
    ffn_rows = exchange(after(ffn_local, out_here), "seq").reshape(ns * rows, 2 * padded)
    ffn_weight = lax.all_gather(ffn_rows, "dp", axis=0, tiled=True)

    chunk_rows = min(CHUNK, piece)
    per_piece = piece // chunk_rows
    order = jnp.stack(
        [
            (((part - me) % ns) * seqs + row) * per_piece + within
            for row in range(seqs)
            for part in range(ns)
            for within in range(per_piece)
        ]
    ).astype(jnp.int32)
    unit_in, scale_in = rms_parts(all_in.astype(F32))
    normed = (unit_in * mixer_gain).astype(BF16)
    projected = dot(normed, mixer_weight).astype(BF16)
    own_cols = lambda table, size: lax.dynamic_slice_in_dim(table, me * size, size, 1)
    filters = jnp.concatenate(
        [own_cols(query_filter, kq), own_cols(key_filter, kq), own_cols(value_filter, kv)], axis=1
    )
    own_decay = jnp.exp(lax.dynamic_slice_in_dim(decay_log, me * heads, heads, 0))
    own_bias = lax.dynamic_slice_in_dim(step_bias, me * heads, heads, 0)
    spread = lambda values: pad_last(
        jnp.stack([jnp.zeros_like(values), values], axis=1).reshape(1, 2 * heads), LANES
    )
    side = jnp.concatenate(
        [spread(own_decay), spread(own_bias), jnp.zeros((6, LANES), F32)], axis=0
    )
    gain_row = head_gain.reshape(1, DV)
    mixed, *saved = mixer_forward(
        projected, filters, side, gain_row, order, heads, seqs, chunk_rows
    )
    all_cot = jnp.concatenate(hand_out([after(flat_cot, projected)] * ns, "seq", -1), axis=0)
    mixed = after(mixed, all_cot)
    mixed_parts = hand_out(mixed.reshape(ns, own, kv), "seq", 1)
    mixed_low = jnp.concatenate(mixed_parts, axis=1)

    middle = flat_in.astype(F32) + dot(mixed_low, turned)
    unit_two, scale_two = rms_parts(middle)
    second_all = ring_gather((unit_two * ffn_gain).astype(BF16), "seq")
    hidden_both = dot(second_all, ffn_weight)
    hidden_gate, hidden_up = hidden_both[:, :padded], hidden_both[:, padded:]
    gate_sig = jax.nn.sigmoid(hidden_gate)
    gate_silu = hidden_gate * gate_sig
    active = (gate_silu * hidden_up).astype(BF16)
    adj_act = dot_nt(all_cot, down_weight)
    adj_gate = adj_act * hidden_up * silu_slope(hidden_gate, gate_sig)
    adj_both = jnp.concatenate(
        [adj_gate.astype(BF16), (adj_act * gate_silu).astype(BF16)], axis=1
    )
    adj_partial_two = dot_nt(adj_both, ffn_weight)
    adj_second, first_in = ring_reduce(adj_partial_two, "seq")
    scatter = lambda grad: lax.psum_scatter(
        grad.astype(BF16), "dp", scatter_dimension=0, tiled=True
    )
    active_late, adj_both_late = after((active, adj_both), first_in)
    ffn_sums = scatter(dot_tn(second_all, adj_both_late))
    grad_down = dot_tn(active_late, all_cot)[:hidden_own].astype(BF16)

    gain_two = jnp.sum(adj_second * unit_two, axis=0)
    adj_middle = flat_cot.astype(F32) + rms_back(unit_two, scale_two, ffn_gain, adj_second)
    attn_low = adj_middle.astype(BF16)
    adj_mixed = dot_nt(attn_low, turned).astype(BF16)
    adj_heads = jnp.concatenate(
        hand_out([adj_mixed[:, hop * kv : (hop + 1) * kv] for hop in range(ns)], "seq", -1), axis=0
    )
    active_late = after(active, adj_mixed)
    block_parts = dot(active_late, down_weight).reshape(ns, own, width)
    mixed_stack = jnp.stack(mixed_parts)
    mixed_natural = jnp.concatenate(
        [take_block(mixed_stack, (me - part) % ns) for part in range(ns)], axis=1
    )
    grad_out = dot_tn(mixed_natural, after(attn_low, adj_mixed)).astype(BF16)
    both_grads = jnp.concatenate(
        [grad_out.reshape(nd, out_rows, width), grad_down.reshape(nd, -1, width)], axis=1
    ).reshape(-1, width)
    both_sums = scatter(both_grads)
    adj_heads = after(adj_heads, both_grads)
    block_low = after(block_parts[1:].astype(BF16), adj_heads)
    block_in = hand_out(
        [block_parts[0]] + [block_low[hop] for hop in range(ns - 1)], "seq", 1
    )
    block_sum = sum(part.astype(F32) for part in block_in[1:]) + block_in[0]
    block_out = (middle + block_sum).astype(BF16).reshape(inputs.shape)
    down_out = both_sums[out_rows:]
    out_sums = both_sums[:out_rows].reshape(ns, -1, width)
    out_out = take_block(out_sums, me).astype(F32)
    out_blocks = [take_block(out_sums, (me + hop) % ns) for hop in range(ns)]
    for part in hand_out(out_blocks, "seq", 1)[1:]:
        out_out = out_out + part.astype(F32)
    out_out = out_out.astype(BF16)
    ffn_parts = exchange(ffn_sums.reshape(ns, rows, -1), "seq")
    ffngate_out = hidden_back(ffn_parts[:, :, :padded], nd, hidden)
    ffnup_out = hidden_back(ffn_parts[:, :, padded:], nd, hidden)

    adj_projected, filter_sum, side_sum, gain_sum = mixer_backward(
        projected, filters, side, gain_row, adj_heads, saved, order, heads, seqs, chunk_rows
    )
    adj_projected = after(adj_projected, block_in[1], block_in[-1])
    adj_partial = dot_nt(adj_projected, mixer_weight)
    gain_one = jnp.sum(adj_partial * unit_in, axis=0)
    adj_normed, first_in = ring_reduce(adj_partial, "seq")
    grad_mixer = dot_tn(normed, after(adj_projected, first_in)).astype(BF16)
    mixer_parts = exchange(scatter(grad_mixer).reshape(ns, rows, -1), "seq")
    whole_rows = lambda parts: jnp.swapaxes(parts, 0, 1).reshape(rows, -1)
    query_out = whole_rows(mixer_parts[:, :, :kq])
    key_out = whole_rows(mixer_parts[:, :, kq : 2 * kq])
    value_out = whole_rows(mixer_parts[:, :, 2 * kq : 2 * kq + kv])
    gate_out = whole_rows(mixer_parts[:, :, 2 * kq + kv : 2 * kq + 2 * kv])
    rate_at = 2 * kq + 2 * kv
    rate_out = whole_rows(mixer_parts[:, :, rate_at : rate_at + 2 * heads])

    unit_one, scale_one = rms_parts(flat_in.astype(F32))
    grad_inputs = (
        (adj_middle + rms_back(unit_one, scale_one, mixer_gain, adj_normed))
        .astype(BF16)
        .reshape(inputs.shape)
    )

    def place(own_part, table, size):
        return lax.dynamic_update_slice_in_dim(
            jnp.zeros(table.shape, F32), own_part, me * size, table.ndim - 1
        )

    small = (
        gain_one,
        gain_two,
        place(filter_sum[:, :kq], query_filter, kq),
        place(filter_sum[:, kq : 2 * kq], key_filter, kq),
        place(filter_sum[:, 2 * kq :], value_filter, kv),
        place(side_sum[0, 1 : 2 * heads : 2], decay_log, heads),
        place(side_sum[1, 1 : 2 * heads : 2], step_bias, heads),
        gain_sum.reshape(DV),
    )
    packed = jnp.concatenate([pad_last(part.reshape(-1), round_up(part.size, LANES)) for part in small])
    packed = sum_everywhere(packed.reshape(-1, LANES)).astype(BF16).reshape(-1)
    outs = []
    at = 0
    for part in small:
        outs.append(packed[at : at + part.size].reshape(part.shape))
        at += round_up(part.size, LANES)
    return (
        block_out,
        grad_inputs,
        query_out,
        key_out,
        value_out,
        gate_out,
        rate_out,
        out_out,
        ffngate_out,
        ffnup_out,
        down_out,
        *outs,
    )


def solution(mesh):
    tokens = P("dp", "seq", None)
    weight = P(("dp", "seq"), None)
    specs = (tokens,) * 2 + (weight,) * 9 + (P(),) * 8
    return jax.shard_map(shards, mesh=mesh, in_specs=specs, out_specs=specs, check_vma=False)
```

```python
import functools

import jax
import jax.numpy as jnp
from jax import lax
from jax.experimental import pallas as pl
from jax.experimental.pallas import tpu as pltpu
from jax.sharding import PartitionSpec as P

H = 8
DK = 128
DV = 256


CHUNK = 256
LANES = 128
F32 = jnp.float32
BF16 = jnp.bfloat16


def mm(left, right, left_dim=1, right_dim=0):
    return lax.dot_general(
        left.astype(BF16),
        right.astype(BF16),
        (((left_dim,), (right_dim,)), ((), ())),
        preferred_element_type=F32,
    )


def mm_nt(left, right):
    return mm(left, right, 1, 1)


def mm_tn(left, right):
    return mm(left, right, 0, 0)


def iota(shape, axis):
    return lax.broadcasted_iota(jnp.int32, shape, axis)


def exact_mm(ones, values):
    first = values.astype(BF16)
    rest = values - first.astype(F32)
    second = rest.astype(BF16)
    third = (rest - second.astype(F32)).astype(BF16)
    return mm(ones, first) + mm(ones, second) + mm(ones, third)


def small_inverses(couplings):
    size = couplings[0].shape[0]
    rows = iota((size, size), 0)
    cols = iota((size, size), 1)
    solved = [jnp.where(rows // 2 == cols // 2, -coupling, 0.0) for coupling in couplings]
    width = 2
    while width < size:
        band = (rows // (2 * width) == cols // (2 * width)) & (rows // width != cols // width)
        parts = [jnp.where(band, coupling, 0.0) for coupling in couplings]
        steps = [part + mm(part, done) for part, done in zip(parts, solved)]
        solved = [done - step - mm(done, step) for done, step in zip(solved, steps)]
        width = 2 * width
    return solved


def lower_inverses(couplings):
    size = couplings[0].shape[0]
    if size <= LANES:
        return small_inverses(couplings)
    half = size // 2
    solved = lower_inverses(
        [coupling[:half, :half] for coupling in couplings]
        + [coupling[half:, half:] for coupling in couplings]
    )
    heads, tails = solved[: len(couplings)], solved[len(couplings) :]
    parts = [coupling[half:, :half] for coupling in couplings]
    steps = [part + mm(part, head) for part, head in zip(parts, heads)]
    corners = [-step - mm(tail, step) for step, tail in zip(steps, tails)]
    blank = jnp.zeros((half, half), F32)
    return [
        jnp.concatenate(
            [
                jnp.concatenate([head, blank], axis=1),
                jnp.concatenate([corner, tail], axis=1),
            ],
            axis=0,
        )
        for head, corner, tail in zip(heads, corners, tails)
    ]


def silu_slope(values, gate):
    return gate * (1.0 + values * (1.0 - gate))


def softplus(values):
    return jnp.maximum(values, 0.0) + jnp.log1p(jnp.exp(-jnp.abs(values)))


def conv_taps(current, before, first_chunk):
    before = jnp.where(first_chunk, 0.0, before.astype(F32))
    joined = jnp.concatenate([before, current.astype(F32)], axis=0)
    top = before.shape[0]
    rows = current.shape[0]
    return [joined[top - 3 + tap : top - 3 + tap + rows] for tap in range(4)]


def decay_parts(rate, decay_scale, decay_bias):
    rows = rate.shape[0]
    shifted = rate + decay_bias
    log_decay = -decay_scale * softplus(shifted)
    lower = jnp.where(iota((rows, rows), 0) >= iota((rows, rows), 1), 1.0, 0.0)
    running = exact_mm(lower, log_decay)
    return shifted, log_decay, running


def head_parts(summed, running, running_rows, head, heads):
    rows = summed.shape[0]
    gates = jax.nn.sigmoid(summed)
    conv = summed * gates
    q_at, k_at, v_at = head * DK, (heads + head) * DK, 2 * heads * DK + head * DV
    q_conv, k_conv = conv[:, q_at : q_at + DK], conv[:, k_at : k_at + DK]
    value = conv[:, v_at : v_at + DV]
    q_scale = lax.rsqrt(jnp.sum(q_conv * q_conv, axis=1, keepdims=True) + 1e-06)
    k_scale = lax.rsqrt(jnp.sum(k_conv * k_conv, axis=1, keepdims=True) + 1e-06)
    query = q_conv * (q_scale * DK**-0.5)
    key = k_conv * k_scale
    lane = 2 * head + 1
    total = running[:, lane : lane + 1]
    across = running_rows[lane : lane + 1, :]
    lower = iota((rows, rows), 0) >= iota((rows, rows), 1)
    decays = jnp.where(lower, jnp.exp(jnp.minimum(total - across, 0.0)), 0.0)
    last = total[rows - 1 : rows, :]
    return q_conv, k_conv, q_scale, k_scale, query, key, value, total, decays, last


def mixer_forward_kernel(
    order_ref, current_ref, before_ref, filter_ref, side_ref, gain_ref,
    mixed_ref, solved_ref, update_ref, start_ref, raw_ref, memory_ref, *, heads
):
    chunk = pl.program_id(1)

    @pl.when(chunk == 0)
    def _():
        memory_ref[...] = jnp.zeros(memory_ref.shape, F32)

    conv_width = 2 * heads * DK + heads * DV
    gate_at = conv_width
    rate_at = conv_width + heads * DV
    taps = conv_taps(
        current_ref[:, :conv_width], before_ref[:, :conv_width], chunk == 0
    )
    rows = taps[0].shape[0]
    summed = taps[0] * filter_ref[0:1, :]
    for tap in range(1, 4):
        summed = summed + taps[tap] * filter_ref[tap : tap + 1, :]
    rate = current_ref[:, rate_at : rate_at + LANES].astype(F32)
    strengths = jax.nn.sigmoid(rate)
    shifted, log_decay, running = decay_parts(rate, side_ref[0:1, :], side_ref[1:2, :])
    running_rows = running.T
    strict = iota((rows, rows), 0) > iota((rows, rows), 1)
    parts = [head_parts(summed, running, running_rows, head, heads) for head in range(heads)]
    inners = [mm_nt(part[5], part[5]) for part in parts]
    solutions = lower_inverses(
        [
            jnp.where(strict, strengths[:, 2 * head : 2 * head + 1] * inner * part[8], 0.0)
            for head, (inner, part) in enumerate(zip(inners, parts))
        ]
    )
    for head in range(heads):
        _, _, _, _, query, key, value, total, decays, last = parts[head]
        strength = strengths[:, 2 * head : 2 * head + 1]
        scaling = jnp.exp(total)
        solved = solutions[head]
        start = memory_ref[head]
        target = strength * (value - scaling * mm(key, start))
        update = target + mm(solved, target)
        scores = mm_nt(query, key) * decays
        raw = scaling * mm(query, start) + mm(scores, update)
        tail = key * jnp.exp(last - total)
        memory_ref[head] = jnp.exp(last) * start + mm_tn(tail, update)
        start_ref[0, 0, head] = start
        solved_ref[0, 0, head] = solved.astype(BF16)
        at = head * DV
        update_ref[:, at : at + DV] = update.astype(BF16)
        raw_ref[:, at : at + DV] = raw
        gate = current_ref[:, gate_at + at : gate_at + at + DV].astype(F32)
        normal = raw * lax.rsqrt(jnp.mean(raw * raw, axis=1, keepdims=True) + 1e-05)
        mixed_ref[:, at : at + DV] = (
            normal * gain_ref[...] * (gate * jax.nn.sigmoid(gate))
        ).astype(BF16)


def mixer_backward_kernel(
    order_ref, current_ref, before_ref, filter_ref, side_ref, gain_ref,
    adjoint_ref, solved_ref, update_ref, start_ref, raw_ref,
    grad_ref, filter_sum_ref, side_sum_ref, gain_sum_ref, memory_ref, after_ref, *, heads, chunks
):
    step = pl.program_id(1)

    @pl.when(step == 0)
    def _():
        memory_ref[...] = jnp.zeros(memory_ref.shape, F32)
        after_ref[...] = jnp.zeros(after_ref.shape, F32)

    @pl.when((step == 0) & (pl.program_id(0) == 0))
    def _():
        filter_sum_ref[...] = jnp.zeros(filter_sum_ref.shape, F32)
        side_sum_ref[...] = jnp.zeros(side_sum_ref.shape, F32)
        gain_sum_ref[...] = jnp.zeros(gain_sum_ref.shape, F32)

    conv_width = 2 * heads * DK + heads * DV
    gate_at = conv_width
    rate_at = conv_width + heads * DV
    taps = conv_taps(
        current_ref[:, :conv_width], before_ref[:, :conv_width], step == chunks - 1
    )
    rows = taps[0].shape[0]
    summed = taps[0] * filter_ref[0:1, :]
    for tap in range(1, 4):
        summed = summed + taps[tap] * filter_ref[tap : tap + 1, :]
    rate = current_ref[:, rate_at : rate_at + LANES].astype(F32)
    strengths = jax.nn.sigmoid(rate)
    decay_scale = side_ref[0:1, :]
    shifted, log_decay, running = decay_parts(rate, decay_scale, side_ref[1:2, :])
    running_rows = running.T
    strict = iota((rows, rows), 0) > iota((rows, rows), 1)
    lane_ids = iota((rows, LANES), 1)
    row_ids = iota((LANES, rows), 0)
    last_lanes = iota((1, LANES), 1)
    sum_across = jnp.zeros((rows, LANES), F32)
    sum_down = jnp.zeros((LANES, rows), F32)
    sum_last = jnp.zeros((1, LANES), F32)
    adj_strength = jnp.zeros((rows, LANES), F32)
    q_adjoints, k_adjoints, v_adjoints = [], [], []
    for head in range(heads):
        q_conv, k_conv, q_scale, k_scale, query, key, value, total, decays, last = head_parts(
            summed, running, running_rows, head, heads
        )
        strength = strengths[:, 2 * head : 2 * head + 1]
        scaling = jnp.exp(total)
        at = head * DV
        raw = raw_ref[:, at : at + DV]
        gate = current_ref[:, gate_at + at : gate_at + at + DV].astype(F32)
        gate_sig = jax.nn.sigmoid(gate)
        gate_silu = gate * gate_sig
        adj_mixed = adjoint_ref[:, at : at + DV].astype(F32)
        inv = lax.rsqrt(jnp.mean(raw * raw, axis=1, keepdims=True) + 1e-05)
        normal = raw * inv
        upstream = adj_mixed * gain_ref[...] * gate_silu
        adj_raw = inv * (
            upstream - normal * jnp.mean(upstream * normal, axis=1, keepdims=True)
        )
        adj_gate = adj_mixed * normal * gain_ref[...] * silu_slope(gate, gate_sig)
        grad_ref[:, gate_at + at : gate_at + at + DV] = adj_gate.astype(BF16)
        gain_sum_ref[...] += jnp.sum(adj_mixed * normal * gate_silu, axis=0, keepdims=True)

        start = start_ref[0, 0, head]
        solved = solved_ref[0, 0, head]
        update = update_ref[:, at : at + DV]
        adj_memory = memory_ref[head]
        tail_decay = jnp.exp(last - total)
        last_decay = jnp.exp(last)
        inner = mm_nt(key, key)
        scores = mm_nt(query, key) * decays
        spread = mm(key * tail_decay, adj_memory)
        adj_update = mm_tn(scores, adj_raw) + spread
        adj_target = adj_update + mm_tn(solved, adj_update)
        adj_scores = mm_nt(adj_raw, update)
        adj_coupling = jnp.where(strict, -mm_nt(adj_target, update), 0.0) * decays
        adj_inner = strength * adj_coupling
        from_inner = adj_coupling * inner
        adj_qk = adj_scores * decays
        key_start = mm(key, start)
        query_start = mm(query, start)
        adj_query = scaling * mm_nt(adj_raw, start) + mm(adj_qk, key)
        adj_key = (
            mm_tn(adj_qk, query)
            + tail_decay * mm_nt(update, adj_memory)
            - scaling * strength * mm_nt(adj_target, start)
            + mm(adj_inner, key)
            + mm_tn(adj_inner, key)
        )
        adj_value = strength * adj_target
        strength_sum = jnp.sum(
            adj_target * (value - scaling * key_start), axis=1, keepdims=True
        ) + jnp.sum(from_inner, axis=1, keepdims=True)
        pairs = adj_scores * scores + strength * from_inner
        tail_sum = jnp.sum(spread * update.astype(F32), axis=1, keepdims=True)
        decay_sum = (
            jnp.sum(pairs, axis=1, keepdims=True)
            + scaling * jnp.sum(query_start * adj_raw, axis=1, keepdims=True)
            - scaling * strength * jnp.sum(key_start * adj_target, axis=1, keepdims=True)
            - tail_sum
        )
        at_end = jnp.sum(tail_sum, axis=0, keepdims=True) + last_decay * jnp.sum(
            jnp.sum(start * adj_memory, axis=1, keepdims=True), axis=0, keepdims=True
        )
        lane = 2 * head + 1
        sum_across = sum_across + jnp.where(lane_ids == lane, decay_sum, 0.0)
        sum_down = sum_down + jnp.where(
            row_ids == lane, jnp.sum(pairs, axis=0, keepdims=True), 0.0
        )
        sum_last = sum_last + jnp.where(last_lanes == lane, at_end, 0.0)
        adj_strength = adj_strength + jnp.where(lane_ids == lane - 1, strength_sum, 0.0)
        memory_ref[head] = (
            last_decay * adj_memory
            + mm_tn(query * scaling, adj_raw)
            - mm_tn(key * (scaling * strength), adj_target)
        )
        adj_query = adj_query * DK**-0.5
        q_adjoints.append(
            q_scale * adj_query
            - q_conv
            * (q_scale * q_scale * q_scale * jnp.sum(q_conv * adj_query, axis=1, keepdims=True))
        )
        k_adjoints.append(
            k_scale * adj_key
            - k_conv
            * (k_scale * k_scale * k_scale * jnp.sum(k_conv * adj_key, axis=1, keepdims=True))
        )
        v_adjoints.append(adj_value)

    upper = jnp.where(iota((rows, rows), 0) <= iota((rows, rows), 1), 1.0, 0.0)
    adj_log_decay = exact_mm(upper, sum_across - sum_down.T) + sum_last
    adj_shifted = -adj_log_decay * decay_scale * jax.nn.sigmoid(shifted)
    adj_rate = adj_shifted + adj_strength * strengths * (1.0 - strengths)
    grad_ref[:, rate_at : rate_at + LANES] = adj_rate.astype(BF16)
    side_sum_ref[0:1, :] += jnp.sum(adj_log_decay * log_decay, axis=0, keepdims=True)
    side_sum_ref[1:2, :] += jnp.sum(adj_shifted, axis=0, keepdims=True)

    adj_conv = jnp.concatenate(q_adjoints + k_adjoints + v_adjoints, axis=1)
    adj_summed = adj_conv * silu_slope(summed, jax.nn.sigmoid(summed))
    joined = jnp.concatenate([adj_summed, after_ref[...]], axis=0)
    after_ref[...] = adj_summed[0:8]
    adj_pre = adj_summed * filter_ref[3:4, :]
    filter_sum_ref[3:4, :] += jnp.sum(adj_summed * taps[3], axis=0, keepdims=True)
    for tap in range(3):
        adj_pre = adj_pre + joined[3 - tap : 3 - tap + rows] * filter_ref[tap : tap + 1, :]
        filter_sum_ref[tap : tap + 1, :] += jnp.sum(adj_summed * taps[tap], axis=0, keepdims=True)
    grad_ref[:, :conv_width] = adj_pre.astype(BF16)


def mixer_call(kernel, order, heads, rows, seqs, chunks, backward, operands, outs, scratch, name):
    ratio = rows // 16
    natural = lambda c: chunks - 1 - c if backward else c
    block = lambda s, c, order_ref: order_ref[s * chunks + natural(c)]

    def before(s, c, order_ref):
        previous = order_ref[s * chunks + jnp.maximum(natural(c) - 1, 0)]
        return (previous * ratio + ratio - 1, 0)

    def spec(array):
        if array.ndim == 5:
            return pl.BlockSpec(
                (1, 1) + array.shape[2:], lambda s, c, order_ref: (s, natural(c), 0, 0, 0)
            )
        if array.shape[0] == rows * seqs * chunks:
            return pl.BlockSpec(
                (rows, array.shape[1]), lambda s, c, order_ref: (block(s, c, order_ref), 0)
            )
        return pl.BlockSpec(array.shape, lambda s, c, order_ref: (0, 0))

    in_specs = [spec(operand) for operand in operands]
    in_specs.insert(1, pl.BlockSpec((16, operands[0].shape[1]), before))
    return pl.pallas_call(
        kernel,
        grid_spec=pltpu.PrefetchScalarGridSpec(
            num_scalar_prefetch=1,
            grid=(seqs, chunks),
            in_specs=in_specs,
            out_specs=[spec(out) for out in outs],
            scratch_shapes=scratch,
        ),
        out_shape=outs,
        compiler_params=pltpu.CompilerParams(vmem_limit_bytes=48 * 1024 * 1024),
        cost_estimate=pl.CostEstimate(
            flops=seqs * chunks * heads * 60 * 2 * rows**3,
            bytes_accessed=24 * 1024 * 1024,
            transcendentals=rows * seqs * chunks * 1024,
        ),
        name=name,
    )(order, operands[0], *operands)


def mixer_forward(projected, filters, side, gain, order, heads, seqs, rows):
    tokens = projected.shape[0]
    chunks = tokens // (rows * seqs)
    shape = jax.ShapeDtypeStruct
    return mixer_call(
        functools.partial(mixer_forward_kernel, heads=heads),
        order, heads, rows, seqs, chunks, False,
        (projected, filters, side, gain),
        [
            shape((tokens, heads * DV), BF16),
            shape((seqs, chunks, heads, rows, rows), BF16),
            shape((tokens, heads * DV), BF16),
            shape((seqs, chunks, heads, DK, DV), F32),
            shape((tokens, heads * DV), F32),
        ],
        [pltpu.VMEM((heads, DK, DV), F32)],
        "mixer_forward",
    )


def mixer_backward(projected, filters, side, gain, adjoint, saved, order, heads, seqs, rows):
    tokens = projected.shape[0]
    chunks = tokens // (rows * seqs)
    shape = jax.ShapeDtypeStruct
    return mixer_call(
        functools.partial(mixer_backward_kernel, heads=heads, chunks=chunks),
        order, heads, rows, seqs, chunks, True,
        (projected, filters, side, gain, adjoint, *saved),
        [
            shape(projected.shape, BF16),
            shape(filters.shape, F32),
            shape((8, LANES), F32),
            shape((1, DV), F32),
        ],
        [pltpu.VMEM((heads, DK, DV), F32), pltpu.VMEM((8, filters.shape[1]), F32)],
        "mixer_backward",
    )


def shift_pairs(count, by):
    return [(place, (place + by) % count) for place in range(count)]


def swap_pairs(count, mask):
    return [(place, place ^ mask) for place in range(count)]


def put_block(whole, block, place):
    return lax.dynamic_update_slice(whole, block[None], (place,) + (0,) * block.ndim)


def near_pieces(block, axis):
    count = lax.axis_size(axis)
    return (
        lax.ppermute(block, axis, shift_pairs(count, 1)),
        lax.ppermute(block, axis, shift_pairs(count, -1)),
    )


def ring_gather(block, axis, near=None):
    count = lax.axis_size(axis)
    found = {0: block}
    right, left = block, block
    for hop in range(1, (count - 1) // 2 + 1):
        if hop == 1:
            right, left = near or near_pieces(block, axis)
        else:
            right = lax.ppermute(right, axis, shift_pairs(count, 1))
            left = lax.ppermute(left, axis, shift_pairs(count, -1))
        found[count - hop] = right
        found[hop] = left
    if count % 2 == 0:
        half = block.shape[0] // 2
        right = lax.ppermute(right[:half], axis, shift_pairs(count, 1))
        left = lax.ppermute(left[half:], axis, shift_pairs(count, -1))
        found[count // 2] = jnp.concatenate([right, left], axis=0)
    return jnp.concatenate([found[hop] for hop in range(count)], axis=0)


def take_block(whole, place):
    return lax.dynamic_index_in_dim(whole, place, 0, keepdims=False)


def ring_reduce(wholes, axis):
    count = lax.axis_size(axis)
    cut = [whole.reshape(count, whole.shape[0] // count, whole.shape[1]) for whole in wholes]
    blocks = [jnp.concatenate([part[hop] for part in cut], axis=0) for hop in range(count)]
    total = blocks[0]
    if count == 1:
        return total, total
    half = total.shape[0] // 2
    first = total
    move = lambda part, by: lax.ppermute(
        part.astype(BF16), axis, shift_pairs(count, by)
    ).astype(F32)
    right = left = None
    if count % 2 == 0:
        far = blocks[count // 2]
        right, left = move(far[:half], 1), move(far[half:], -1)
        first = right
    for hop in range((count - 1) // 2, 0, -1):
        ahead, behind = blocks[hop], blocks[count - hop]
        if right is not None and right.shape[0] == half:
            ahead = jnp.concatenate([ahead[:half] + right, ahead[half:]], axis=0)
            behind = jnp.concatenate([behind[:half], behind[half:] + left], axis=0)
        elif right is not None:
            ahead, behind = ahead + right, behind + left
        right, left = move(ahead, 1), move(behind, -1)
    if right.shape[0] == half:
        return total + jnp.concatenate([right, left], axis=0), first
    return total + right + left, first


def hand_out(blocks, axis, by):
    count = lax.axis_size(axis)
    return [blocks[0]] + [
        lax.ppermute(blocks[hop], axis, shift_pairs(count, hop * by)) for hop in range(1, count)
    ]


def exchange(whole, axis):
    count = lax.axis_size(axis)
    me = lax.axis_index(axis)
    result = put_block(jnp.zeros(whole.shape, whole.dtype), take_block(whole, me), me)
    for hop in range(1, count):
        moved = lax.ppermute(
            take_block(whole, (me + hop) % count), axis, shift_pairs(count, hop)
        )
        result = put_block(result, moved, (me - hop) % count)
    return result


def after(values, *others):
    return lax.optimization_barrier((values, *others))[0]


def sum_everywhere(values):
    for axis in ("dp", "seq"):
        count = lax.axis_size(axis)
        if count & (count - 1):
            values = lax.psum(values, axis)
            continue
        mask = 1
        while mask < count:
            values = values + lax.ppermute(values, axis, swap_pairs(count, mask))
            mask *= 2
    return values


def round_up(size, step):
    return (size + step - 1) // step * step


def rms_parts(values):
    scale = lax.rsqrt(jnp.mean(values * values, axis=-1, keepdims=True) + 1e-05)
    return values * scale, scale


def rms_back(unit, scale, gain, adjoint):
    scaled = adjoint * gain
    return scale * (scaled - unit * jnp.mean(scaled * unit, axis=-1, keepdims=True))


def dot(left, right):
    return jnp.dot(left, right, preferred_element_type=F32)


def dot_nt(left, right):
    return jnp.einsum("tc,dc->td", left, right, preferred_element_type=F32)


def dot_tn(left, right):
    return jnp.einsum("tr,tc->rc", left, right, preferred_element_type=F32)


def by_heads(weight, ns):
    return jnp.swapaxes(weight.reshape(weight.shape[0], ns, weight.shape[1] // ns), 0, 1)


def pad_last(values, size):
    if values.shape[-1] == size:
        return values
    return jnp.pad(values, [(0, 0)] * (values.ndim - 1) + [(0, size - values.shape[-1])])


def hidden_out(weight, nd, ns, padded):
    rows, hidden = weight.shape
    block = hidden // (nd * ns)
    parts = jnp.transpose(weight.reshape(rows, nd, ns, block), (2, 0, 1, 3))
    return pad_last(parts.reshape(ns, rows, nd * block), padded)


def hidden_back(parts, nd, hidden):
    ns, rows, _ = parts.shape
    block = hidden // (nd * ns)
    kept = parts[:, :, : nd * block].reshape(ns, rows, nd, block)
    return jnp.transpose(kept, (1, 2, 0, 3)).reshape(rows, hidden)


def shards(
    inputs,
    cotangent,
    query_proj,
    key_proj,
    value_proj,
    gate_proj,
    rate_proj,
    output_proj,
    ffn_gate,
    ffn_up,
    ffn_down,
    mixer_gain,
    ffn_gain,
    query_filter,
    key_filter,
    value_filter,
    decay_log,
    step_bias,
    head_gain,
):
    seqs, piece, width = inputs.shape
    ns, nd = lax.axis_size("seq"), lax.axis_size("dp")
    me = lax.axis_index("seq")
    heads = H // ns
    kq, kv = heads * DK, heads * DV
    own = seqs * piece
    tokens = own * ns
    rows = query_proj.shape[0]
    hidden = ffn_gate.shape[1]
    hidden_own = hidden // ns
    padded = round_up(hidden_own, LANES)

    flat_in = inputs.reshape(own, width)
    flat_cot = cotangent.reshape(own, width)
    mixer_local = jnp.concatenate(
        [by_heads(w, ns) for w in (query_proj, key_proj, value_proj, gate_proj)]
        + [pad_last(by_heads(rate_proj, ns), LANES)],
        axis=2,
    )
    mixer_width = mixer_local.shape[2]
    ffn_local = jnp.concatenate(
        [hidden_out(ffn_gate, nd, ns, padded), hidden_out(ffn_up, nd, ns, padded)], axis=2
    )
    out_local = jnp.broadcast_to(output_proj.reshape(1, rows, -1), (ns, rows, output_proj.size // rows))
    near = near_pieces(flat_in, "seq")
    mixer_rows = exchange(mixer_local, "seq").reshape(ns * rows, mixer_width)
    mixer_rows, near = lax.optimization_barrier((mixer_rows, near))
    mixer_weight = lax.all_gather(mixer_rows, "dp", axis=0, tiled=True)
    all_in = ring_gather(flat_in, "seq", near)
    shared = exchange(after(jnp.concatenate([ffn_local, out_local], axis=2), near), "seq")
    out_rows = ns * output_proj.shape[0]
    out_here = shared[:, :, 2 * padded :].reshape(out_rows, width)
    down_rows = ffn_down.shape[0]
    spare = jnp.zeros((-(out_rows + down_rows) % 16, width), BF16)
    both = jnp.concatenate([out_here, ffn_down, spare], axis=0)
    both = lax.all_gather(both, "dp", axis=0, tiled=False)
    out_weight = both[:, :out_rows].reshape(ns, kv, width)
    turned = jnp.concatenate([take_block(out_weight, (me - hop) % ns) for hop in range(ns)], axis=0)
    down_weight = both[:, out_rows : out_rows + down_rows].reshape(hidden_own, width)
    down_weight = jnp.pad(down_weight, ((0, padded - hidden_own), (0, 0)))
    ffn_rows = shared[:, :, : 2 * padded].reshape(ns * rows, 2 * padded)
    ffn_weight = lax.all_gather(ffn_rows, "dp", axis=0, tiled=True)

    chunk_rows = min(CHUNK, piece)
    per_piece = piece // chunk_rows
    order = jnp.stack(
        [
            (((part - me) % ns) * seqs + row) * per_piece + within
            for row in range(seqs)
            for part in range(ns)
            for within in range(per_piece)
        ]
    ).astype(jnp.int32)
    unit_in, scale_in = rms_parts(all_in.astype(F32))
    normed = (unit_in * mixer_gain).astype(BF16)
    projected = dot(normed, mixer_weight).astype(BF16)
    own_cols = lambda table, size: lax.dynamic_slice_in_dim(table, me * size, size, 1)
    filters = jnp.concatenate(
        [own_cols(query_filter, kq), own_cols(key_filter, kq), own_cols(value_filter, kv)], axis=1
    )
    own_decay = jnp.exp(lax.dynamic_slice_in_dim(decay_log, me * heads, heads, 0))
    own_bias = lax.dynamic_slice_in_dim(step_bias, me * heads, heads, 0)
    spread = lambda values: pad_last(
        jnp.stack([jnp.zeros_like(values), values], axis=1).reshape(1, 2 * heads), LANES
    )
    side = jnp.concatenate(
        [spread(own_decay), spread(own_bias), jnp.zeros((6, LANES), F32)], axis=0
    )
    gain_row = head_gain.reshape(1, DV)
    mixed, *saved = mixer_forward(
        projected, filters, side, gain_row, order, heads, seqs, chunk_rows
    )
    cot_near = near_pieces(after(flat_cot, projected), "seq")
    mixed, cot_near = lax.optimization_barrier((mixed, cot_near))
    all_cot = ring_gather(flat_cot, "seq", cot_near)
    mixed_parts = hand_out(mixed.reshape(ns, own, kv), "seq", 1)
    mixed_low = jnp.concatenate(mixed_parts, axis=1)

    middle = flat_in.astype(F32) + dot(mixed_low, turned)
    unit_two, scale_two = rms_parts(middle)
    second_all = ring_gather((unit_two * ffn_gain).astype(BF16), "seq")
    hidden_both = dot(second_all, ffn_weight)
    hidden_gate, hidden_up = hidden_both[:, :padded], hidden_both[:, padded:]
    gate_sig = jax.nn.sigmoid(hidden_gate)
    gate_silu = hidden_gate * gate_sig
    active = (gate_silu * hidden_up).astype(BF16)
    adj_act = dot_nt(all_cot, down_weight)
    adj_gate = adj_act * hidden_up * silu_slope(hidden_gate, gate_sig)
    adj_both = jnp.concatenate(
        [adj_gate.astype(BF16), (adj_act * gate_silu).astype(BF16)], axis=1
    )
    adj_partial_two = dot_nt(adj_both, ffn_weight)
    adj_second, first_in = ring_reduce([adj_partial_two], "seq")
    scatter = lambda grad: lax.psum_scatter(
        grad.astype(BF16), "dp", scatter_dimension=0, tiled=True
    )
    active_late, adj_both_late = after((active, adj_both), first_in)
    grad_ffn = dot_tn(second_all, adj_both_late).astype(BF16)
    ffn_sums = scatter(grad_ffn)
    adj_second = after(adj_second, grad_ffn)
    grad_down = dot_tn(active_late, all_cot)[:hidden_own].astype(BF16)

    gain_two = jnp.sum(adj_second * unit_two, axis=0)
    adj_middle = flat_cot.astype(F32) + rms_back(unit_two, scale_two, ffn_gain, adj_second)
    attn_low = adj_middle.astype(BF16)
    attn_near = near_pieces(attn_low, "seq")
    active_late = after(active, attn_low)
    block_parts = dot(active_late, down_weight)
    attn_all = ring_gather(attn_low, "seq", attn_near)
    adj_heads = dot_nt(attn_all, take_block(out_weight, me)).astype(BF16)
    grad_out = dot_tn(mixed, attn_all).astype(BF16)
    head_rows = kv // nd
    spare = jnp.zeros((nd, -(head_rows + down_rows) % 16, width), BF16)
    both_grads = jnp.concatenate(
        [
            grad_out.reshape(nd, head_rows, width),
            grad_down.reshape(nd, down_rows, width),
            spare,
        ],
        axis=1,
    ).reshape(-1, width)
    both_sums = scatter(both_grads)
    adj_heads = after(adj_heads, both_grads, ffn_sums)
    down_out = both_sums[head_rows : head_rows + down_rows]
    owners = [
        (place * ns + part, part * nd + place) for place in range(nd) for part in range(ns)
    ]
    out_out = lax.ppermute(both_sums[:head_rows], ("dp", "seq"), owners)

    adj_projected, filter_sum, side_sum, gain_sum = mixer_backward(
        projected, filters, side, gain_row, adj_heads, saved, order, heads, seqs, chunk_rows
    )
    grad_mixer = dot_tn(normed, adj_projected).astype(BF16)
    mixer_sums = scatter(after(grad_mixer, both_sums))
    adj_partial = dot_nt(after(adj_projected, grad_mixer), mixer_weight)
    gain_one = jnp.sum(adj_partial * unit_in, axis=0)
    reduced, _ = ring_reduce([adj_partial, block_parts], "seq")
    adj_normed, block_sum = reduced[:own], reduced[own:]
    block_out = (middle + block_sum).astype(BF16).reshape(inputs.shape)
    shared = jnp.concatenate(
        [mixer_sums.reshape(ns, rows, -1), ffn_sums.reshape(ns, rows, -1)], axis=2
    )
    shared = exchange(shared, "seq")
    mixer_parts, ffn_parts = shared[:, :, :-2 * padded], shared[:, :, -2 * padded:]
    ffngate_out = hidden_back(ffn_parts[:, :, :padded], nd, hidden)
    ffnup_out = hidden_back(ffn_parts[:, :, padded:], nd, hidden)
    whole_rows = lambda parts: jnp.swapaxes(parts, 0, 1).reshape(rows, -1)
    query_out = whole_rows(mixer_parts[:, :, :kq])
    key_out = whole_rows(mixer_parts[:, :, kq : 2 * kq])
    value_out = whole_rows(mixer_parts[:, :, 2 * kq : 2 * kq + kv])
    gate_out = whole_rows(mixer_parts[:, :, 2 * kq + kv : 2 * kq + 2 * kv])
    rate_at = 2 * kq + 2 * kv
    rate_out = whole_rows(mixer_parts[:, :, rate_at : rate_at + 2 * heads])

    unit_one, scale_one = rms_parts(flat_in.astype(F32))
    grad_inputs = (
        (adj_middle + rms_back(unit_one, scale_one, mixer_gain, adj_normed))
        .astype(BF16)
        .reshape(inputs.shape)
    )

    def place(own_part, table, size):
        return lax.dynamic_update_slice_in_dim(
            jnp.zeros(table.shape, F32), own_part, me * size, table.ndim - 1
        )

    small = (
        gain_one,
        gain_two,
        place(filter_sum[:, :kq], query_filter, kq),
        place(filter_sum[:, kq : 2 * kq], key_filter, kq),
        place(filter_sum[:, 2 * kq :], value_filter, kv),
        place(side_sum[0, 1 : 2 * heads : 2], decay_log, heads),
        place(side_sum[1, 1 : 2 * heads : 2], step_bias, heads),
        gain_sum.reshape(DV),
    )
    packed = jnp.concatenate([pad_last(part.reshape(-1), round_up(part.size, LANES)) for part in small])
    packed = sum_everywhere(packed.reshape(-1, LANES)).astype(BF16).reshape(-1)
    outs = []
    at = 0
    for part in small:
        outs.append(packed[at : at + part.size].reshape(part.shape))
        at += round_up(part.size, LANES)
    return (
        block_out,
        grad_inputs,
        query_out,
        key_out,
        value_out,
        gate_out,
        rate_out,
        out_out,
        ffngate_out,
        ffnup_out,
        down_out,
        *outs,
    )


def solution(mesh):
    tokens = P("dp", "seq", None)
    weight = P(("dp", "seq"), None)
    specs = (tokens,) * 2 + (weight,) * 9 + (P(),) * 8
    return jax.shard_map(shards, mesh=mesh, in_specs=specs, out_specs=specs, check_vma=False)
```

```python
import functools

import jax
import jax.numpy as jnp
from jax import lax
from jax.experimental import pallas as pl
from jax.experimental.pallas import tpu as pltpu
from jax.sharding import PartitionSpec as P

H = 8
DK = 128
DV = 256


CHUNK = 256
LANES = 128
F32 = jnp.float32
BF16 = jnp.bfloat16


def mm(left, right, left_dim=1, right_dim=0):
    return lax.dot_general(
        left.astype(BF16),
        right.astype(BF16),
        (((left_dim,), (right_dim,)), ((), ())),
        preferred_element_type=F32,
    )


def mm_nt(left, right):
    return mm(left, right, 1, 1)


def mm_tn(left, right):
    return mm(left, right, 0, 0)


def iota(shape, axis):
    return lax.broadcasted_iota(jnp.int32, shape, axis)


def exact_mm(ones, values):
    first = values.astype(BF16)
    rest = values - first.astype(F32)
    second = rest.astype(BF16)
    third = (rest - second.astype(F32)).astype(BF16)
    return mm(ones, first) + mm(ones, second) + mm(ones, third)


def small_inverses(couplings):
    size = couplings[0].shape[0]
    rows = iota((size, size), 0)
    cols = iota((size, size), 1)
    solved = [jnp.where(rows // 2 == cols // 2, -coupling, 0.0) for coupling in couplings]
    width = 2
    while width < size:
        band = (rows // (2 * width) == cols // (2 * width)) & (rows // width != cols // width)
        parts = [jnp.where(band, coupling, 0.0) for coupling in couplings]
        steps = [part + mm(part, done) for part, done in zip(parts, solved)]
        solved = [done - step - mm(done, step) for done, step in zip(solved, steps)]
        width = 2 * width
    return solved


def lower_inverses(couplings):
    size = couplings[0].shape[0]
    if size <= LANES:
        return small_inverses(couplings)
    half = size // 2
    solved = lower_inverses(
        [coupling[:half, :half] for coupling in couplings]
        + [coupling[half:, half:] for coupling in couplings]
    )
    heads, tails = solved[: len(couplings)], solved[len(couplings) :]
    parts = [coupling[half:, :half] for coupling in couplings]
    steps = [part + mm(part, head) for part, head in zip(parts, heads)]
    corners = [-step - mm(tail, step) for step, tail in zip(steps, tails)]
    blank = jnp.zeros((half, half), F32)
    return [
        jnp.concatenate(
            [
                jnp.concatenate([head, blank], axis=1),
                jnp.concatenate([corner, tail], axis=1),
            ],
            axis=0,
        )
        for head, corner, tail in zip(heads, corners, tails)
    ]


def silu_slope(values, gate):
    return gate * (1.0 + values * (1.0 - gate))


def softplus(values):
    return jnp.maximum(values, 0.0) + jnp.log1p(jnp.exp(-jnp.abs(values)))


def conv_taps(current, before, first_chunk):
    before = jnp.where(first_chunk, 0.0, before.astype(F32))
    joined = jnp.concatenate([before, current.astype(F32)], axis=0)
    top = before.shape[0]
    rows = current.shape[0]
    return [joined[top - 3 + tap : top - 3 + tap + rows] for tap in range(4)]


def decay_parts(rate, decay_scale, decay_bias):
    rows = rate.shape[0]
    shifted = rate + decay_bias
    log_decay = -decay_scale * softplus(shifted)
    lower = jnp.where(iota((rows, rows), 0) >= iota((rows, rows), 1), 1.0, 0.0)
    running = exact_mm(lower, log_decay)
    return shifted, log_decay, running


def head_parts(summed, running, running_rows, head, heads):
    rows = summed.shape[0]
    gates = jax.nn.sigmoid(summed)
    conv = summed * gates
    q_at, k_at, v_at = head * DK, (heads + head) * DK, 2 * heads * DK + head * DV
    q_conv, k_conv = conv[:, q_at : q_at + DK], conv[:, k_at : k_at + DK]
    value = conv[:, v_at : v_at + DV]
    q_scale = lax.rsqrt(jnp.sum(q_conv * q_conv, axis=1, keepdims=True) + 1e-06)
    k_scale = lax.rsqrt(jnp.sum(k_conv * k_conv, axis=1, keepdims=True) + 1e-06)
    query = q_conv * (q_scale * DK**-0.5)
    key = k_conv * k_scale
    lane = 2 * head + 1
    total = running[:, lane : lane + 1]
    across = running_rows[lane : lane + 1, :]
    lower = iota((rows, rows), 0) >= iota((rows, rows), 1)
    decays = jnp.where(lower, jnp.exp(jnp.minimum(total - across, 0.0)), 0.0)
    last = total[rows - 1 : rows, :]
    return q_conv, k_conv, q_scale, k_scale, query, key, value, total, decays, last


def mixer_forward_kernel(
    order_ref, current_ref, before_ref, filter_ref, side_ref, gain_ref,
    mixed_ref, solved_ref, update_ref, start_ref, raw_ref, memory_ref, *, heads
):
    chunk = pl.program_id(1)

    @pl.when(chunk == 0)
    def _():
        memory_ref[...] = jnp.zeros(memory_ref.shape, F32)

    conv_width = 2 * heads * DK + heads * DV
    gate_at = conv_width
    rate_at = conv_width + heads * DV
    taps = conv_taps(
        current_ref[:, :conv_width], before_ref[:, :conv_width], chunk == 0
    )
    rows = taps[0].shape[0]
    summed = taps[0] * filter_ref[0:1, :]
    for tap in range(1, 4):
        summed = summed + taps[tap] * filter_ref[tap : tap + 1, :]
    rate = current_ref[:, rate_at : rate_at + LANES].astype(F32)
    strengths = jax.nn.sigmoid(rate)
    shifted, log_decay, running = decay_parts(rate, side_ref[0:1, :], side_ref[1:2, :])
    running_rows = running.T
    strict = iota((rows, rows), 0) > iota((rows, rows), 1)
    parts = [head_parts(summed, running, running_rows, head, heads) for head in range(heads)]
    inners = [mm_nt(part[5], part[5]) for part in parts]
    solutions = lower_inverses(
        [
            jnp.where(strict, strengths[:, 2 * head : 2 * head + 1] * inner * part[8], 0.0)
            for head, (inner, part) in enumerate(zip(inners, parts))
        ]
    )
    for head in range(heads):
        _, _, _, _, query, key, value, total, decays, last = parts[head]
        strength = strengths[:, 2 * head : 2 * head + 1]
        scaling = jnp.exp(total)
        solved = solutions[head]
        start = memory_ref[head]
        target = strength * (value - scaling * mm(key, start))
        update = target + mm(solved, target)
        scores = mm_nt(query, key) * decays
        raw = scaling * mm(query, start) + mm(scores, update)
        tail = key * jnp.exp(last - total)
        memory_ref[head] = jnp.exp(last) * start + mm_tn(tail, update)
        start_ref[0, 0, head] = start
        solved_ref[0, 0, head] = solved.astype(BF16)
        at = head * DV
        update_ref[:, at : at + DV] = update.astype(BF16)
        raw_ref[:, at : at + DV] = raw
        gate = current_ref[:, gate_at + at : gate_at + at + DV].astype(F32)
        normal = raw * lax.rsqrt(jnp.mean(raw * raw, axis=1, keepdims=True) + 1e-05)
        mixed_ref[:, at : at + DV] = (
            normal * gain_ref[...] * (gate * jax.nn.sigmoid(gate))
        ).astype(BF16)


def mixer_backward_kernel(
    order_ref, current_ref, before_ref, filter_ref, side_ref, gain_ref,
    adjoint_ref, solved_ref, update_ref, start_ref, raw_ref,
    grad_ref, filter_sum_ref, side_sum_ref, gain_sum_ref, memory_ref, after_ref, *, heads, chunks
):
    step = pl.program_id(1)

    @pl.when(step == 0)
    def _():
        memory_ref[...] = jnp.zeros(memory_ref.shape, F32)
        after_ref[...] = jnp.zeros(after_ref.shape, F32)

    @pl.when((step == 0) & (pl.program_id(0) == 0))
    def _():
        filter_sum_ref[...] = jnp.zeros(filter_sum_ref.shape, F32)
        side_sum_ref[...] = jnp.zeros(side_sum_ref.shape, F32)
        gain_sum_ref[...] = jnp.zeros(gain_sum_ref.shape, F32)

    conv_width = 2 * heads * DK + heads * DV
    gate_at = conv_width
    rate_at = conv_width + heads * DV
    taps = conv_taps(
        current_ref[:, :conv_width], before_ref[:, :conv_width], step == chunks - 1
    )
    rows = taps[0].shape[0]
    summed = taps[0] * filter_ref[0:1, :]
    for tap in range(1, 4):
        summed = summed + taps[tap] * filter_ref[tap : tap + 1, :]
    rate = current_ref[:, rate_at : rate_at + LANES].astype(F32)
    strengths = jax.nn.sigmoid(rate)
    decay_scale = side_ref[0:1, :]
    shifted, log_decay, running = decay_parts(rate, decay_scale, side_ref[1:2, :])
    running_rows = running.T
    strict = iota((rows, rows), 0) > iota((rows, rows), 1)
    lane_ids = iota((rows, LANES), 1)
    row_ids = iota((LANES, rows), 0)
    last_lanes = iota((1, LANES), 1)
    sum_across = jnp.zeros((rows, LANES), F32)
    sum_down = jnp.zeros((LANES, rows), F32)
    sum_last = jnp.zeros((1, LANES), F32)
    adj_strength = jnp.zeros((rows, LANES), F32)
    q_adjoints, k_adjoints, v_adjoints = [], [], []
    for head in range(heads):
        q_conv, k_conv, q_scale, k_scale, query, key, value, total, decays, last = head_parts(
            summed, running, running_rows, head, heads
        )
        strength = strengths[:, 2 * head : 2 * head + 1]
        scaling = jnp.exp(total)
        at = head * DV
        raw = raw_ref[:, at : at + DV]
        gate = current_ref[:, gate_at + at : gate_at + at + DV].astype(F32)
        gate_sig = jax.nn.sigmoid(gate)
        gate_silu = gate * gate_sig
        adj_mixed = adjoint_ref[:, at : at + DV].astype(F32)
        inv = lax.rsqrt(jnp.mean(raw * raw, axis=1, keepdims=True) + 1e-05)
        normal = raw * inv
        upstream = adj_mixed * gain_ref[...] * gate_silu
        adj_raw = inv * (
            upstream - normal * jnp.mean(upstream * normal, axis=1, keepdims=True)
        )
        adj_gate = adj_mixed * normal * gain_ref[...] * silu_slope(gate, gate_sig)
        grad_ref[:, gate_at + at : gate_at + at + DV] = adj_gate.astype(BF16)
        gain_sum_ref[...] += jnp.sum(adj_mixed * normal * gate_silu, axis=0, keepdims=True)

        start = start_ref[0, 0, head]
        solved = solved_ref[0, 0, head]
        update = update_ref[:, at : at + DV]
        adj_memory = memory_ref[head]
        tail_decay = jnp.exp(last - total)
        last_decay = jnp.exp(last)
        inner = mm_nt(key, key)
        scores = mm_nt(query, key) * decays
        spread = mm(key * tail_decay, adj_memory)
        adj_update = mm_tn(scores, adj_raw) + spread
        adj_target = adj_update + mm_tn(solved, adj_update)
        adj_scores = mm_nt(adj_raw, update)
        adj_coupling = jnp.where(strict, -mm_nt(adj_target, update), 0.0) * decays
        adj_inner = strength * adj_coupling
        from_inner = adj_coupling * inner
        adj_qk = adj_scores * decays
        key_start = mm(key, start)
        query_start = mm(query, start)
        adj_query = scaling * mm_nt(adj_raw, start) + mm(adj_qk, key)
        adj_key = (
            mm_tn(adj_qk, query)
            + tail_decay * mm_nt(update, adj_memory)
            - scaling * strength * mm_nt(adj_target, start)
            + mm(adj_inner, key)
            + mm_tn(adj_inner, key)
        )
        adj_value = strength * adj_target
        strength_sum = jnp.sum(
            adj_target * (value - scaling * key_start), axis=1, keepdims=True
        ) + jnp.sum(from_inner, axis=1, keepdims=True)
        pairs = adj_scores * scores + strength * from_inner
        tail_sum = jnp.sum(spread * update.astype(F32), axis=1, keepdims=True)
        decay_sum = (
            jnp.sum(pairs, axis=1, keepdims=True)
            + scaling * jnp.sum(query_start * adj_raw, axis=1, keepdims=True)
            - scaling * strength * jnp.sum(key_start * adj_target, axis=1, keepdims=True)
            - tail_sum
        )
        at_end = jnp.sum(tail_sum, axis=0, keepdims=True) + last_decay * jnp.sum(
            jnp.sum(start * adj_memory, axis=1, keepdims=True), axis=0, keepdims=True
        )
        lane = 2 * head + 1
        sum_across = sum_across + jnp.where(lane_ids == lane, decay_sum, 0.0)
        sum_down = sum_down + jnp.where(
            row_ids == lane, jnp.sum(pairs, axis=0, keepdims=True), 0.0
        )
        sum_last = sum_last + jnp.where(last_lanes == lane, at_end, 0.0)
        adj_strength = adj_strength + jnp.where(lane_ids == lane - 1, strength_sum, 0.0)
        memory_ref[head] = (
            last_decay * adj_memory
            + mm_tn(query * scaling, adj_raw)
            - mm_tn(key * (scaling * strength), adj_target)
        )
        adj_query = adj_query * DK**-0.5
        q_adjoints.append(
            q_scale * adj_query
            - q_conv
            * (q_scale * q_scale * q_scale * jnp.sum(q_conv * adj_query, axis=1, keepdims=True))
        )
        k_adjoints.append(
            k_scale * adj_key
            - k_conv
            * (k_scale * k_scale * k_scale * jnp.sum(k_conv * adj_key, axis=1, keepdims=True))
        )
        v_adjoints.append(adj_value)

    upper = jnp.where(iota((rows, rows), 0) <= iota((rows, rows), 1), 1.0, 0.0)
    adj_log_decay = exact_mm(upper, sum_across - sum_down.T) + sum_last
    adj_shifted = -adj_log_decay * decay_scale * jax.nn.sigmoid(shifted)
    adj_rate = adj_shifted + adj_strength * strengths * (1.0 - strengths)
    grad_ref[:, rate_at : rate_at + LANES] = adj_rate.astype(BF16)
    side_sum_ref[0:1, :] += jnp.sum(adj_log_decay * log_decay, axis=0, keepdims=True)
    side_sum_ref[1:2, :] += jnp.sum(adj_shifted, axis=0, keepdims=True)

    adj_conv = jnp.concatenate(q_adjoints + k_adjoints + v_adjoints, axis=1)
    adj_summed = adj_conv * silu_slope(summed, jax.nn.sigmoid(summed))
    joined = jnp.concatenate([adj_summed, after_ref[...]], axis=0)
    after_ref[...] = adj_summed[0:8]
    adj_pre = adj_summed * filter_ref[3:4, :]
    filter_sum_ref[3:4, :] += jnp.sum(adj_summed * taps[3], axis=0, keepdims=True)
    for tap in range(3):
        adj_pre = adj_pre + joined[3 - tap : 3 - tap + rows] * filter_ref[tap : tap + 1, :]
        filter_sum_ref[tap : tap + 1, :] += jnp.sum(adj_summed * taps[tap], axis=0, keepdims=True)
    grad_ref[:, :conv_width] = adj_pre.astype(BF16)


def mixer_call(kernel, order, heads, rows, seqs, chunks, backward, operands, outs, scratch, name):
    ratio = rows // 16
    natural = lambda c: chunks - 1 - c if backward else c
    block = lambda s, c, order_ref: order_ref[s * chunks + natural(c)]

    def before(s, c, order_ref):
        previous = order_ref[s * chunks + jnp.maximum(natural(c) - 1, 0)]
        return (previous * ratio + ratio - 1, 0)

    def spec(array):
        if array.ndim == 5:
            return pl.BlockSpec(
                (1, 1) + array.shape[2:], lambda s, c, order_ref: (s, natural(c), 0, 0, 0)
            )
        if array.shape[0] == rows * seqs * chunks:
            return pl.BlockSpec(
                (rows, array.shape[1]), lambda s, c, order_ref: (block(s, c, order_ref), 0)
            )
        return pl.BlockSpec(array.shape, lambda s, c, order_ref: (0, 0))

    in_specs = [spec(operand) for operand in operands]
    in_specs.insert(1, pl.BlockSpec((16, operands[0].shape[1]), before))
    return pl.pallas_call(
        kernel,
        grid_spec=pltpu.PrefetchScalarGridSpec(
            num_scalar_prefetch=1,
            grid=(seqs, chunks),
            in_specs=in_specs,
            out_specs=[spec(out) for out in outs],
            scratch_shapes=scratch,
        ),
        out_shape=outs,
        compiler_params=pltpu.CompilerParams(vmem_limit_bytes=48 * 1024 * 1024),
        cost_estimate=pl.CostEstimate(
            flops=seqs * chunks * heads * 60 * 2 * rows**3,
            bytes_accessed=24 * 1024 * 1024,
            transcendentals=rows * seqs * chunks * 1024,
        ),
        name=name,
    )(order, operands[0], *operands)


def mixer_forward(projected, filters, side, gain, order, heads, seqs, rows):
    tokens = projected.shape[0]
    chunks = tokens // (rows * seqs)
    shape = jax.ShapeDtypeStruct
    return mixer_call(
        functools.partial(mixer_forward_kernel, heads=heads),
        order, heads, rows, seqs, chunks, False,
        (projected, filters, side, gain),
        [
            shape((tokens, heads * DV), BF16),
            shape((seqs, chunks, heads, rows, rows), BF16),
            shape((tokens, heads * DV), BF16),
            shape((seqs, chunks, heads, DK, DV), F32),
            shape((tokens, heads * DV), F32),
        ],
        [pltpu.VMEM((heads, DK, DV), F32)],
        "mixer_forward",
    )


def mixer_backward(projected, filters, side, gain, adjoint, saved, order, heads, seqs, rows):
    tokens = projected.shape[0]
    chunks = tokens // (rows * seqs)
    shape = jax.ShapeDtypeStruct
    return mixer_call(
        functools.partial(mixer_backward_kernel, heads=heads, chunks=chunks),
        order, heads, rows, seqs, chunks, True,
        (projected, filters, side, gain, adjoint, *saved),
        [
            shape(projected.shape, BF16),
            shape(filters.shape, F32),
            shape((8, LANES), F32),
            shape((1, DV), F32),
        ],
        [pltpu.VMEM((heads, DK, DV), F32), pltpu.VMEM((8, filters.shape[1]), F32)],
        "mixer_backward",
    )


def shift_pairs(count, by):
    return [(place, (place + by) % count) for place in range(count)]


def swap_pairs(count, mask):
    return [(place, place ^ mask) for place in range(count)]


def put_block(whole, block, place):
    return lax.dynamic_update_slice(whole, block[None], (place,) + (0,) * block.ndim)


def near_pieces(block, axis):
    count = lax.axis_size(axis)
    return (
        lax.ppermute(block, axis, shift_pairs(count, 1)),
        lax.ppermute(block, axis, shift_pairs(count, -1)),
    )


def ring_gather(block, axis, near=None):
    count = lax.axis_size(axis)
    found = {0: block}
    right, left = block, block
    for hop in range(1, (count - 1) // 2 + 1):
        if hop == 1:
            right, left = near or near_pieces(block, axis)
        else:
            right = lax.ppermute(right, axis, shift_pairs(count, 1))
            left = lax.ppermute(left, axis, shift_pairs(count, -1))
        found[count - hop] = right
        found[hop] = left
    if count % 2 == 0:
        half = block.shape[0] // 2
        right = lax.ppermute(right[:half], axis, shift_pairs(count, 1))
        left = lax.ppermute(left[half:], axis, shift_pairs(count, -1))
        found[count // 2] = jnp.concatenate([right, left], axis=0)
    return jnp.concatenate([found[hop] for hop in range(count)], axis=0)


def take_block(whole, place):
    return lax.dynamic_index_in_dim(whole, place, 0, keepdims=False)


def ring_reduce(wholes, axis):
    count = lax.axis_size(axis)
    cut = [whole.reshape(count, whole.shape[0] // count, whole.shape[1]) for whole in wholes]
    blocks = [jnp.concatenate([part[hop] for part in cut], axis=0) for hop in range(count)]
    total = blocks[0]
    if count == 1:
        return total, total
    half = total.shape[0] // 2
    first = total
    move = lambda part, by: lax.ppermute(
        part.astype(BF16), axis, shift_pairs(count, by)
    ).astype(F32)
    right = left = None
    if count % 2 == 0:
        far = blocks[count // 2]
        right, left = move(far[:half], 1), move(far[half:], -1)
        first = right
    for hop in range((count - 1) // 2, 0, -1):
        ahead, behind = blocks[hop], blocks[count - hop]
        if right is not None and right.shape[0] == half:
            ahead = jnp.concatenate([ahead[:half] + right, ahead[half:]], axis=0)
            behind = jnp.concatenate([behind[:half], behind[half:] + left], axis=0)
        elif right is not None:
            ahead, behind = ahead + right, behind + left
        right, left = move(ahead, 1), move(behind, -1)
    if right.shape[0] == half:
        return total + jnp.concatenate([right, left], axis=0), first
    return total + right + left, first


def hand_out(blocks, axis, by):
    count = lax.axis_size(axis)
    return [blocks[0]] + [
        lax.ppermute(blocks[hop], axis, shift_pairs(count, hop * by)) for hop in range(1, count)
    ]


def exchange(whole, axis):
    count = lax.axis_size(axis)
    me = lax.axis_index(axis)
    result = put_block(jnp.zeros(whole.shape, whole.dtype), take_block(whole, me), me)
    for hop in range(1, count):
        moved = lax.ppermute(
            take_block(whole, (me + hop) % count), axis, shift_pairs(count, hop)
        )
        result = put_block(result, moved, (me - hop) % count)
    return result


def together(*values):
    return lax.optimization_barrier(values)


def sum_everywhere(values):
    for axis in ("dp", "seq"):
        count = lax.axis_size(axis)
        if count & (count - 1):
            values = lax.psum(values, axis)
            continue
        mask = 1
        while mask < count:
            values = values + lax.ppermute(values, axis, swap_pairs(count, mask))
            mask *= 2
    return values


def round_up(size, step):
    return (size + step - 1) // step * step


def rms_parts(values):
    scale = lax.rsqrt(jnp.mean(values * values, axis=-1, keepdims=True) + 1e-05)
    return values * scale, scale


def rms_back(unit, scale, gain, adjoint):
    scaled = adjoint * gain
    return scale * (scaled - unit * jnp.mean(scaled * unit, axis=-1, keepdims=True))


def dot(left, right):
    return jnp.dot(left, right, preferred_element_type=F32)


def dot_nt(left, right):
    return jnp.einsum("tc,dc->td", left, right, preferred_element_type=F32)


def dot_tn(left, right):
    return jnp.einsum("tr,tc->rc", left, right, preferred_element_type=F32)


def by_heads(weight, ns):
    return jnp.swapaxes(weight.reshape(weight.shape[0], ns, weight.shape[1] // ns), 0, 1)


def pad_last(values, size):
    if values.shape[-1] == size:
        return values
    return jnp.pad(values, [(0, 0)] * (values.ndim - 1) + [(0, size - values.shape[-1])])


def hidden_out(weight, nd, ns, padded):
    rows, hidden = weight.shape
    block = hidden // (nd * ns)
    parts = jnp.transpose(weight.reshape(rows, nd, ns, block), (2, 0, 1, 3))
    return pad_last(parts.reshape(ns, rows, nd * block), padded)


def hidden_back(parts, nd, hidden):
    ns, rows, _ = parts.shape
    block = hidden // (nd * ns)
    kept = parts[:, :, : nd * block].reshape(ns, rows, nd, block)
    return jnp.transpose(kept, (1, 2, 0, 3)).reshape(rows, hidden)


def shards(
    inputs,
    cotangent,
    query_proj,
    key_proj,
    value_proj,
    gate_proj,
    rate_proj,
    output_proj,
    ffn_gate,
    ffn_up,
    ffn_down,
    mixer_gain,
    ffn_gain,
    query_filter,
    key_filter,
    value_filter,
    decay_log,
    step_bias,
    head_gain,
):
    seqs, piece, width = inputs.shape
    ns, nd = lax.axis_size("seq"), lax.axis_size("dp")
    me = lax.axis_index("seq")
    heads = H // ns
    kq, kv = heads * DK, heads * DV
    own = seqs * piece
    tokens = own * ns
    rows = query_proj.shape[0]
    hidden = ffn_gate.shape[1]
    hidden_own = hidden // ns
    padded = round_up(hidden_own, LANES)

    flat_in = inputs.reshape(own, width)
    flat_cot = cotangent.reshape(own, width)
    mixer_local = jnp.concatenate(
        [by_heads(w, ns) for w in (query_proj, key_proj, value_proj, gate_proj)]
        + [pad_last(by_heads(rate_proj, ns), LANES)],
        axis=2,
    )
    mixer_width = mixer_local.shape[2]
    ffn_local = jnp.concatenate(
        [hidden_out(ffn_gate, nd, ns, padded), hidden_out(ffn_up, nd, ns, padded)], axis=2
    )
    out_local = jnp.broadcast_to(output_proj.reshape(1, rows, -1), (ns, rows, output_proj.size // rows))
    near = near_pieces(flat_in, "seq")
    mixer_rows = exchange(mixer_local, "seq").reshape(ns * rows, mixer_width)
    mixer_rows, near = lax.optimization_barrier((mixer_rows, near))
    mixer_weight = lax.all_gather(mixer_rows, "dp", axis=0, tiled=True)
    all_in = ring_gather(flat_in, "seq", near)
    second_local, all_in = together(jnp.concatenate([ffn_local, out_local], axis=2), all_in)
    shared = exchange(second_local, "seq")
    out_rows = ns * output_proj.shape[0]
    out_here = shared[:, :, 2 * padded :].reshape(out_rows, width)
    down_rows = ffn_down.shape[0]
    spare = jnp.zeros((-(out_rows + down_rows) % 16, width), BF16)
    both = jnp.concatenate([out_here, ffn_down, spare], axis=0)
    both = lax.all_gather(both, "dp", axis=0, tiled=False)
    out_weight = both[:, :out_rows].reshape(ns, kv, width)
    turned = jnp.concatenate([take_block(out_weight, (me - hop) % ns) for hop in range(ns)], axis=0)
    down_weight = both[:, out_rows : out_rows + down_rows].reshape(hidden_own, width)
    down_weight = jnp.pad(down_weight, ((0, padded - hidden_own), (0, 0)))
    ffn_rows = shared[:, :, : 2 * padded].reshape(ns * rows, 2 * padded)
    ffn_weight = lax.all_gather(ffn_rows, "dp", axis=0, tiled=True)

    chunk_rows = min(CHUNK, piece)
    per_piece = piece // chunk_rows
    order = jnp.stack(
        [
            (((part - me) % ns) * seqs + row) * per_piece + within
            for row in range(seqs)
            for part in range(ns)
            for within in range(per_piece)
        ]
    ).astype(jnp.int32)
    unit_in, scale_in = rms_parts(all_in.astype(F32))
    normed = (unit_in * mixer_gain).astype(BF16)
    projected = dot(normed, mixer_weight).astype(BF16)
    own_cols = lambda table, size: lax.dynamic_slice_in_dim(table, me * size, size, 1)
    filters = jnp.concatenate(
        [own_cols(query_filter, kq), own_cols(key_filter, kq), own_cols(value_filter, kv)], axis=1
    )
    own_decay = jnp.exp(lax.dynamic_slice_in_dim(decay_log, me * heads, heads, 0))
    own_bias = lax.dynamic_slice_in_dim(step_bias, me * heads, heads, 0)
    spread = lambda values: pad_last(
        jnp.stack([jnp.zeros_like(values), values], axis=1).reshape(1, 2 * heads), LANES
    )
    side = jnp.concatenate(
        [spread(own_decay), spread(own_bias), jnp.zeros((6, LANES), F32)], axis=0
    )
    gain_row = head_gain.reshape(1, DV)
    mixed, *saved = mixer_forward(
        projected, filters, side, gain_row, order, heads, seqs, chunk_rows
    )
    late_cot, projected = together(flat_cot, projected)
    cot_near = near_pieces(late_cot, "seq")
    mixed, cot_near = together(mixed, cot_near)
    all_cot = ring_gather(flat_cot, "seq", cot_near)
    mixed_parts = hand_out(mixed.reshape(ns, own, kv), "seq", 1)
    mixed_low = jnp.concatenate(mixed_parts, axis=1)

    middle = flat_in.astype(F32) + dot(mixed_low, turned)
    unit_two, scale_two = rms_parts(middle)
    second_all = ring_gather((unit_two * ffn_gain).astype(BF16), "seq")
    hidden_both = dot(second_all, ffn_weight)
    hidden_gate, hidden_up = hidden_both[:, :padded], hidden_both[:, padded:]
    gate_sig = jax.nn.sigmoid(hidden_gate)
    gate_silu = hidden_gate * gate_sig
    active = (gate_silu * hidden_up).astype(BF16)
    adj_act = dot_nt(all_cot, down_weight)
    adj_gate = adj_act * hidden_up * silu_slope(hidden_gate, gate_sig)
    adj_both = jnp.concatenate(
        [adj_gate.astype(BF16), (adj_act * gate_silu).astype(BF16)], axis=1
    )
    adj_partial_two = dot_nt(adj_both, ffn_weight)
    scatter = lambda grad: lax.psum_scatter(
        grad.astype(BF16), "dp", scatter_dimension=0, tiled=True
    )
    adj_both_late, adj_partial_two = together(adj_both, adj_partial_two)
    grad_ffn = dot_tn(second_all, adj_both_late).astype(BF16)
    adj_second, first_in = ring_reduce([adj_partial_two], "seq")
    grad_ffn, adj_second = together(grad_ffn, adj_second)
    ffn_sums = scatter(grad_ffn)

    gain_two = jnp.sum(adj_second * unit_two, axis=0)
    adj_middle = flat_cot.astype(F32) + rms_back(unit_two, scale_two, ffn_gain, adj_second)
    attn_low = adj_middle.astype(BF16)
    active_late, attn_low = together(active, attn_low)
    attn_near = near_pieces(attn_low, "seq")
    block_parts = dot(active_late, down_weight)
    grad_down = dot_tn(active_late, all_cot)[:hidden_own].astype(BF16)
    attn_near, block_parts, grad_down = together(attn_near, block_parts, grad_down)
    attn_all = ring_gather(attn_low, "seq", attn_near)
    adj_heads = dot_nt(attn_all, take_block(out_weight, me)).astype(BF16)
    grad_out = dot_tn(mixed, attn_all).astype(BF16)
    head_rows = kv // nd
    spare = jnp.zeros((nd, -(head_rows + down_rows) % 16, width), BF16)
    both_grads = jnp.concatenate(
        [
            grad_out.reshape(nd, head_rows, width),
            grad_down.reshape(nd, down_rows, width),
            spare,
        ],
        axis=1,
    ).reshape(-1, width)
    adj_heads, both_grads, ffn_sums = together(adj_heads, both_grads, ffn_sums)
    both_sums = scatter(both_grads)
    down_out = both_sums[head_rows : head_rows + down_rows]
    owners = [
        (place * ns + part, part * nd + place) for place in range(nd) for part in range(ns)
    ]
    out_out = lax.ppermute(both_sums[:head_rows], ("dp", "seq"), owners)

    adj_projected, filter_sum, side_sum, gain_sum = mixer_backward(
        projected, filters, side, gain_row, adj_heads, saved, order, heads, seqs, chunk_rows
    )
    grad_mixer = dot_tn(normed, adj_projected).astype(BF16)
    adj_projected, grad_mixer = together(adj_projected, grad_mixer)
    mixer_sums = scatter(grad_mixer)
    adj_partial = dot_nt(adj_projected, mixer_weight)
    gain_one = jnp.sum(adj_partial * unit_in, axis=0)
    reduced, _ = ring_reduce([adj_partial, block_parts], "seq")
    adj_normed, block_sum = reduced[:own], reduced[own:]
    gain_one, adj_normed = together(gain_one, adj_normed)
    block_out = (middle + block_sum).astype(BF16).reshape(inputs.shape)
    shared = jnp.concatenate(
        [mixer_sums.reshape(ns, rows, -1), ffn_sums.reshape(ns, rows, -1)], axis=2
    )
    shared = exchange(shared, "seq")
    mixer_parts, ffn_parts = shared[:, :, :-2 * padded], shared[:, :, -2 * padded:]
    ffngate_out = hidden_back(ffn_parts[:, :, :padded], nd, hidden)
    ffnup_out = hidden_back(ffn_parts[:, :, padded:], nd, hidden)
    whole_rows = lambda parts: jnp.swapaxes(parts, 0, 1).reshape(rows, -1)
    query_out = whole_rows(mixer_parts[:, :, :kq])
    key_out = whole_rows(mixer_parts[:, :, kq : 2 * kq])
    value_out = whole_rows(mixer_parts[:, :, 2 * kq : 2 * kq + kv])
    gate_out = whole_rows(mixer_parts[:, :, 2 * kq + kv : 2 * kq + 2 * kv])
    rate_at = 2 * kq + 2 * kv
    rate_out = whole_rows(mixer_parts[:, :, rate_at : rate_at + 2 * heads])

    unit_one, scale_one = rms_parts(flat_in.astype(F32))
    grad_inputs = (
        (adj_middle + rms_back(unit_one, scale_one, mixer_gain, adj_normed))
        .astype(BF16)
        .reshape(inputs.shape)
    )

    def place(own_part, table, size):
        return lax.dynamic_update_slice_in_dim(
            jnp.zeros(table.shape, F32), own_part, me * size, table.ndim - 1
        )

    small = (
        gain_one,
        gain_two,
        place(filter_sum[:, :kq], query_filter, kq),
        place(filter_sum[:, kq : 2 * kq], key_filter, kq),
        place(filter_sum[:, 2 * kq :], value_filter, kv),
        place(side_sum[0, 1 : 2 * heads : 2], decay_log, heads),
        place(side_sum[1, 1 : 2 * heads : 2], step_bias, heads),
        gain_sum.reshape(DV),
    )
    packed = jnp.concatenate([pad_last(part.reshape(-1), round_up(part.size, LANES)) for part in small])
    packed = sum_everywhere(packed.reshape(-1, LANES)).astype(BF16).reshape(-1)
    outs = []
    at = 0
    for part in small:
        outs.append(packed[at : at + part.size].reshape(part.shape))
        at += round_up(part.size, LANES)
    return (
        block_out,
        grad_inputs,
        query_out,
        key_out,
        value_out,
        gate_out,
        rate_out,
        out_out,
        ffngate_out,
        ffnup_out,
        down_out,
        *outs,
    )


def solution(mesh):
    tokens = P("dp", "seq", None)
    weight = P(("dp", "seq"), None)
    specs = (tokens,) * 2 + (weight,) * 9 + (P(),) * 8
    return jax.shard_map(shards, mesh=mesh, in_specs=specs, out_specs=specs, check_vma=False)
```

```python
import functools

import jax
import jax.numpy as jnp
from jax import lax
from jax.experimental import pallas as pl
from jax.experimental.pallas import tpu as pltpu
from jax.sharding import PartitionSpec as P

H = 8
DK = 128
DV = 256


CHUNK = 256
LANES = 128
F32 = jnp.float32
BF16 = jnp.bfloat16


def mm(left, right, left_dim=1, right_dim=0):
    return lax.dot_general(
        left.astype(BF16),
        right.astype(BF16),
        (((left_dim,), (right_dim,)), ((), ())),
        preferred_element_type=F32,
    )


def mm_nt(left, right):
    return mm(left, right, 1, 1)


def mm_tn(left, right):
    return mm(left, right, 0, 0)


def iota(shape, axis):
    return lax.broadcasted_iota(jnp.int32, shape, axis)


def exact_mm(ones, values):
    first = values.astype(BF16)
    rest = values - first.astype(F32)
    second = rest.astype(BF16)
    third = (rest - second.astype(F32)).astype(BF16)
    return mm(ones, first) + mm(ones, second) + mm(ones, third)


def small_inverses(couplings):
    size = couplings[0].shape[0]
    rows = iota((size, size), 0)
    cols = iota((size, size), 1)
    solved = [jnp.where(rows // 2 == cols // 2, -coupling, 0.0) for coupling in couplings]
    width = 2
    while width < size:
        band = (rows // (2 * width) == cols // (2 * width)) & (rows // width != cols // width)
        parts = [jnp.where(band, coupling, 0.0) for coupling in couplings]
        steps = [part + mm(part, done) for part, done in zip(parts, solved)]
        solved = [done - step - mm(done, step) for done, step in zip(solved, steps)]
        width = 2 * width
    return solved


def lower_inverses(couplings):
    size = couplings[0].shape[0]
    if size <= LANES:
        return small_inverses(couplings)
    half = size // 2
    solved = lower_inverses(
        [coupling[:half, :half] for coupling in couplings]
        + [coupling[half:, half:] for coupling in couplings]
    )
    heads, tails = solved[: len(couplings)], solved[len(couplings) :]
    parts = [coupling[half:, :half] for coupling in couplings]
    steps = [part + mm(part, head) for part, head in zip(parts, heads)]
    corners = [-step - mm(tail, step) for step, tail in zip(steps, tails)]
    blank = jnp.zeros((half, half), F32)
    return [
        jnp.concatenate(
            [
                jnp.concatenate([head, blank], axis=1),
                jnp.concatenate([corner, tail], axis=1),
            ],
            axis=0,
        )
        for head, corner, tail in zip(heads, corners, tails)
    ]


def silu_slope(values, gate):
    return gate * (1.0 + values * (1.0 - gate))


def softplus(values):
    return jnp.maximum(values, 0.0) + jnp.log1p(jnp.exp(-jnp.abs(values)))


def conv_taps(current, before, first_chunk):
    before = jnp.where(first_chunk, 0.0, before.astype(F32))
    joined = jnp.concatenate([before, current.astype(F32)], axis=0)
    top = before.shape[0]
    rows = current.shape[0]
    return [joined[top - 3 + tap : top - 3 + tap + rows] for tap in range(4)]


def decay_parts(rate, decay_scale, decay_bias):
    rows = rate.shape[0]
    shifted = rate + decay_bias
    log_decay = -decay_scale * softplus(shifted)
    lower = jnp.where(iota((rows, rows), 0) >= iota((rows, rows), 1), 1.0, 0.0)
    running = exact_mm(lower, log_decay)
    return shifted, log_decay, running


def head_parts(summed, running, running_rows, head, heads):
    rows = summed.shape[0]
    gates = jax.nn.sigmoid(summed)
    conv = summed * gates
    q_at, k_at, v_at = head * DK, (heads + head) * DK, 2 * heads * DK + head * DV
    q_conv, k_conv = conv[:, q_at : q_at + DK], conv[:, k_at : k_at + DK]
    value = conv[:, v_at : v_at + DV]
    q_scale = lax.rsqrt(jnp.sum(q_conv * q_conv, axis=1, keepdims=True) + 1e-06)
    k_scale = lax.rsqrt(jnp.sum(k_conv * k_conv, axis=1, keepdims=True) + 1e-06)
    query = q_conv * (q_scale * DK**-0.5)
    key = k_conv * k_scale
    lane = 2 * head + 1
    total = running[:, lane : lane + 1]
    across = running_rows[lane : lane + 1, :]
    lower = iota((rows, rows), 0) >= iota((rows, rows), 1)
    decays = jnp.where(lower, jnp.exp(jnp.minimum(total - across, 0.0)), 0.0)
    last = total[rows - 1 : rows, :]
    return q_conv, k_conv, q_scale, k_scale, query, key, value, total, decays, last


def mixer_forward_kernel(
    order_ref, current_ref, before_ref, filter_ref, side_ref, gain_ref,
    mixed_ref, solved_ref, update_ref, start_ref, raw_ref, memory_ref, *, heads
):
    chunk = pl.program_id(1)

    @pl.when(chunk == 0)
    def _():
        memory_ref[...] = jnp.zeros(memory_ref.shape, F32)

    conv_width = 2 * heads * DK + heads * DV
    gate_at = conv_width
    rate_at = conv_width + heads * DV
    taps = conv_taps(
        current_ref[:, :conv_width], before_ref[:, :conv_width], chunk == 0
    )
    rows = taps[0].shape[0]
    summed = taps[0] * filter_ref[0:1, :]
    for tap in range(1, 4):
        summed = summed + taps[tap] * filter_ref[tap : tap + 1, :]
    rate = current_ref[:, rate_at : rate_at + LANES].astype(F32)
    strengths = jax.nn.sigmoid(rate)
    shifted, log_decay, running = decay_parts(rate, side_ref[0:1, :], side_ref[1:2, :])
    running_rows = running.T
    strict = iota((rows, rows), 0) > iota((rows, rows), 1)
    parts = [head_parts(summed, running, running_rows, head, heads) for head in range(heads)]
    inners = [mm_nt(part[5], part[5]) for part in parts]
    solutions = lower_inverses(
        [
            jnp.where(strict, strengths[:, 2 * head : 2 * head + 1] * inner * part[8], 0.0)
            for head, (inner, part) in enumerate(zip(inners, parts))
        ]
    )
    for head in range(heads):
        _, _, _, _, query, key, value, total, decays, last = parts[head]
        strength = strengths[:, 2 * head : 2 * head + 1]
        scaling = jnp.exp(total)
        solved = solutions[head]
        start = memory_ref[head]
        target = strength * (value - scaling * mm(key, start))
        update = target + mm(solved, target)
        scores = mm_nt(query, key) * decays
        raw = scaling * mm(query, start) + mm(scores, update)
        tail = key * jnp.exp(last - total)
        memory_ref[head] = jnp.exp(last) * start + mm_tn(tail, update)
        start_ref[0, 0, head] = start
        solved_ref[0, 0, head] = solved.astype(BF16)
        at = head * DV
        update_ref[:, at : at + DV] = update.astype(BF16)
        raw_ref[:, at : at + DV] = raw
        gate = current_ref[:, gate_at + at : gate_at + at + DV].astype(F32)
        normal = raw * lax.rsqrt(jnp.mean(raw * raw, axis=1, keepdims=True) + 1e-05)
        mixed_ref[:, at : at + DV] = (
            normal * gain_ref[...] * (gate * jax.nn.sigmoid(gate))
        ).astype(BF16)


def mixer_backward_kernel(
    order_ref, current_ref, before_ref, filter_ref, side_ref, gain_ref,
    adjoint_ref, solved_ref, update_ref, start_ref, raw_ref,
    grad_ref, filter_sum_ref, side_sum_ref, gain_sum_ref, memory_ref, after_ref, *, heads, chunks
):
    step = pl.program_id(1)

    @pl.when(step == 0)
    def _():
        memory_ref[...] = jnp.zeros(memory_ref.shape, F32)
        after_ref[...] = jnp.zeros(after_ref.shape, F32)

    @pl.when((step == 0) & (pl.program_id(0) == 0))
    def _():
        filter_sum_ref[...] = jnp.zeros(filter_sum_ref.shape, F32)
        side_sum_ref[...] = jnp.zeros(side_sum_ref.shape, F32)
        gain_sum_ref[...] = jnp.zeros(gain_sum_ref.shape, F32)

    conv_width = 2 * heads * DK + heads * DV
    gate_at = conv_width
    rate_at = conv_width + heads * DV
    taps = conv_taps(
        current_ref[:, :conv_width], before_ref[:, :conv_width], step == chunks - 1
    )
    rows = taps[0].shape[0]
    summed = taps[0] * filter_ref[0:1, :]
    for tap in range(1, 4):
        summed = summed + taps[tap] * filter_ref[tap : tap + 1, :]
    rate = current_ref[:, rate_at : rate_at + LANES].astype(F32)
    strengths = jax.nn.sigmoid(rate)
    decay_scale = side_ref[0:1, :]
    shifted, log_decay, running = decay_parts(rate, decay_scale, side_ref[1:2, :])
    running_rows = running.T
    strict = iota((rows, rows), 0) > iota((rows, rows), 1)
    lane_ids = iota((rows, LANES), 1)
    row_ids = iota((LANES, rows), 0)
    last_lanes = iota((1, LANES), 1)
    sum_across = jnp.zeros((rows, LANES), F32)
    sum_down = jnp.zeros((LANES, rows), F32)
    sum_last = jnp.zeros((1, LANES), F32)
    adj_strength = jnp.zeros((rows, LANES), F32)
    q_adjoints, k_adjoints, v_adjoints = [], [], []
    for head in range(heads):
        q_conv, k_conv, q_scale, k_scale, query, key, value, total, decays, last = head_parts(
            summed, running, running_rows, head, heads
        )
        strength = strengths[:, 2 * head : 2 * head + 1]
        scaling = jnp.exp(total)
        at = head * DV
        raw = raw_ref[:, at : at + DV]
        gate = current_ref[:, gate_at + at : gate_at + at + DV].astype(F32)
        gate_sig = jax.nn.sigmoid(gate)
        gate_silu = gate * gate_sig
        adj_mixed = adjoint_ref[:, at : at + DV].astype(F32)
        inv = lax.rsqrt(jnp.mean(raw * raw, axis=1, keepdims=True) + 1e-05)
        normal = raw * inv
        upstream = adj_mixed * gain_ref[...] * gate_silu
        adj_raw = inv * (
            upstream - normal * jnp.mean(upstream * normal, axis=1, keepdims=True)
        )
        adj_gate = adj_mixed * normal * gain_ref[...] * silu_slope(gate, gate_sig)
        grad_ref[:, gate_at + at : gate_at + at + DV] = adj_gate.astype(BF16)
        gain_sum_ref[...] += jnp.sum(adj_mixed * normal * gate_silu, axis=0, keepdims=True)

        start = start_ref[0, 0, head]
        solved = solved_ref[0, 0, head]
        update = update_ref[:, at : at + DV]
        adj_memory = memory_ref[head]
        tail_decay = jnp.exp(last - total)
        last_decay = jnp.exp(last)
        inner = mm_nt(key, key)
        scores = mm_nt(query, key) * decays
        spread = mm(key * tail_decay, adj_memory)
        adj_update = mm_tn(scores, adj_raw) + spread
        adj_target = adj_update + mm_tn(solved, adj_update)
        adj_scores = mm_nt(adj_raw, update)
        adj_coupling = jnp.where(strict, -mm_nt(adj_target, update), 0.0) * decays
        adj_inner = strength * adj_coupling
        from_inner = adj_coupling * inner
        adj_qk = adj_scores * decays
        key_start = mm(key, start)
        query_start = mm(query, start)
        adj_query = scaling * mm_nt(adj_raw, start) + mm(adj_qk, key)
        adj_key = (
            mm_tn(adj_qk, query)
            + tail_decay * mm_nt(update, adj_memory)
            - scaling * strength * mm_nt(adj_target, start)
            + mm(adj_inner, key)
            + mm_tn(adj_inner, key)
        )
        adj_value = strength * adj_target
        strength_sum = jnp.sum(
            adj_target * (value - scaling * key_start), axis=1, keepdims=True
        ) + jnp.sum(from_inner, axis=1, keepdims=True)
        pairs = adj_scores * scores + strength * from_inner
        tail_sum = jnp.sum(spread * update.astype(F32), axis=1, keepdims=True)
        decay_sum = (
            jnp.sum(pairs, axis=1, keepdims=True)
            + scaling * jnp.sum(query_start * adj_raw, axis=1, keepdims=True)
            - scaling * strength * jnp.sum(key_start * adj_target, axis=1, keepdims=True)
            - tail_sum
        )
        at_end = jnp.sum(tail_sum, axis=0, keepdims=True) + last_decay * jnp.sum(
            jnp.sum(start * adj_memory, axis=1, keepdims=True), axis=0, keepdims=True
        )
        lane = 2 * head + 1
        sum_across = sum_across + jnp.where(lane_ids == lane, decay_sum, 0.0)
        sum_down = sum_down + jnp.where(
            row_ids == lane, jnp.sum(pairs, axis=0, keepdims=True), 0.0
        )
        sum_last = sum_last + jnp.where(last_lanes == lane, at_end, 0.0)
        adj_strength = adj_strength + jnp.where(lane_ids == lane - 1, strength_sum, 0.0)
        memory_ref[head] = (
            last_decay * adj_memory
            + mm_tn(query * scaling, adj_raw)
            - mm_tn(key * (scaling * strength), adj_target)
        )
        adj_query = adj_query * DK**-0.5
        q_adjoints.append(
            q_scale * adj_query
            - q_conv
            * (q_scale * q_scale * q_scale * jnp.sum(q_conv * adj_query, axis=1, keepdims=True))
        )
        k_adjoints.append(
            k_scale * adj_key
            - k_conv
            * (k_scale * k_scale * k_scale * jnp.sum(k_conv * adj_key, axis=1, keepdims=True))
        )
        v_adjoints.append(adj_value)

    upper = jnp.where(iota((rows, rows), 0) <= iota((rows, rows), 1), 1.0, 0.0)
    adj_log_decay = exact_mm(upper, sum_across - sum_down.T) + sum_last
    adj_shifted = -adj_log_decay * decay_scale * jax.nn.sigmoid(shifted)
    adj_rate = adj_shifted + adj_strength * strengths * (1.0 - strengths)
    grad_ref[:, rate_at : rate_at + LANES] = adj_rate.astype(BF16)
    side_sum_ref[0:1, :] += jnp.sum(adj_log_decay * log_decay, axis=0, keepdims=True)
    side_sum_ref[1:2, :] += jnp.sum(adj_shifted, axis=0, keepdims=True)

    adj_conv = jnp.concatenate(q_adjoints + k_adjoints + v_adjoints, axis=1)
    adj_summed = adj_conv * silu_slope(summed, jax.nn.sigmoid(summed))
    joined = jnp.concatenate([adj_summed, after_ref[...]], axis=0)
    after_ref[...] = adj_summed[0:8]
    adj_pre = adj_summed * filter_ref[3:4, :]
    filter_sum_ref[3:4, :] += jnp.sum(adj_summed * taps[3], axis=0, keepdims=True)
    for tap in range(3):
        adj_pre = adj_pre + joined[3 - tap : 3 - tap + rows] * filter_ref[tap : tap + 1, :]
        filter_sum_ref[tap : tap + 1, :] += jnp.sum(adj_summed * taps[tap], axis=0, keepdims=True)
    grad_ref[:, :conv_width] = adj_pre.astype(BF16)


def mixer_call(kernel, order, heads, rows, seqs, chunks, backward, operands, outs, scratch, name):
    ratio = rows // 16
    natural = lambda c: chunks - 1 - c if backward else c
    block = lambda s, c, order_ref: order_ref[s * chunks + natural(c)]

    def before(s, c, order_ref):
        previous = order_ref[s * chunks + jnp.maximum(natural(c) - 1, 0)]
        return (previous * ratio + ratio - 1, 0)

    def spec(array):
        if array.ndim == 5:
            return pl.BlockSpec(
                (1, 1) + array.shape[2:], lambda s, c, order_ref: (s, natural(c), 0, 0, 0)
            )
        if array.shape[0] == rows * seqs * chunks:
            return pl.BlockSpec(
                (rows, array.shape[1]), lambda s, c, order_ref: (block(s, c, order_ref), 0)
            )
        return pl.BlockSpec(array.shape, lambda s, c, order_ref: (0, 0))

    in_specs = [spec(operand) for operand in operands]
    in_specs.insert(1, pl.BlockSpec((16, operands[0].shape[1]), before))
    return pl.pallas_call(
        kernel,
        grid_spec=pltpu.PrefetchScalarGridSpec(
            num_scalar_prefetch=1,
            grid=(seqs, chunks),
            in_specs=in_specs,
            out_specs=[spec(out) for out in outs],
            scratch_shapes=scratch,
        ),
        out_shape=outs,
        compiler_params=pltpu.CompilerParams(vmem_limit_bytes=48 * 1024 * 1024),
        cost_estimate=pl.CostEstimate(
            flops=seqs * chunks * heads * 60 * 2 * rows**3,
            bytes_accessed=24 * 1024 * 1024,
            transcendentals=rows * seqs * chunks * 1024,
        ),
        name=name,
    )(order, operands[0], *operands)


def mixer_forward(projected, filters, side, gain, order, heads, seqs, rows):
    tokens = projected.shape[0]
    chunks = tokens // (rows * seqs)
    shape = jax.ShapeDtypeStruct
    return mixer_call(
        functools.partial(mixer_forward_kernel, heads=heads),
        order, heads, rows, seqs, chunks, False,
        (projected, filters, side, gain),
        [
            shape((tokens, heads * DV), BF16),
            shape((seqs, chunks, heads, rows, rows), BF16),
            shape((tokens, heads * DV), BF16),
            shape((seqs, chunks, heads, DK, DV), F32),
            shape((tokens, heads * DV), F32),
        ],
        [pltpu.VMEM((heads, DK, DV), F32)],
        "mixer_forward",
    )


def mixer_backward(projected, filters, side, gain, adjoint, saved, order, heads, seqs, rows):
    tokens = projected.shape[0]
    chunks = tokens // (rows * seqs)
    shape = jax.ShapeDtypeStruct
    return mixer_call(
        functools.partial(mixer_backward_kernel, heads=heads, chunks=chunks),
        order, heads, rows, seqs, chunks, True,
        (projected, filters, side, gain, adjoint, *saved),
        [
            shape(projected.shape, BF16),
            shape(filters.shape, F32),
            shape((8, LANES), F32),
            shape((1, DV), F32),
        ],
        [pltpu.VMEM((heads, DK, DV), F32), pltpu.VMEM((8, filters.shape[1]), F32)],
        "mixer_backward",
    )


def shift_pairs(count, by):
    return [(place, (place + by) % count) for place in range(count)]


def swap_pairs(count, mask):
    return [(place, place ^ mask) for place in range(count)]


def put_block(whole, block, place):
    return lax.dynamic_update_slice(whole, block[None], (place,) + (0,) * block.ndim)


def near_pieces(block, axis):
    count = lax.axis_size(axis)
    return (
        lax.ppermute(block, axis, shift_pairs(count, 1)),
        lax.ppermute(block, axis, shift_pairs(count, -1)),
    )


def ring_gather(block, axis, near=None):
    count = lax.axis_size(axis)
    found = {0: block}
    right, left = block, block
    for hop in range(1, (count - 1) // 2 + 1):
        if hop == 1:
            right, left = near or near_pieces(block, axis)
        else:
            right = lax.ppermute(right, axis, shift_pairs(count, 1))
            left = lax.ppermute(left, axis, shift_pairs(count, -1))
        found[count - hop] = right
        found[hop] = left
    if count % 2 == 0:
        half = block.shape[0] // 2
        right = lax.ppermute(right[:half], axis, shift_pairs(count, 1))
        left = lax.ppermute(left[half:], axis, shift_pairs(count, -1))
        found[count // 2] = jnp.concatenate([right, left], axis=0)
    return jnp.concatenate([found[hop] for hop in range(count)], axis=0)


def take_block(whole, place):
    return lax.dynamic_index_in_dim(whole, place, 0, keepdims=False)


def ring_reduce(wholes, axis):
    count = lax.axis_size(axis)
    cut = [whole.reshape(count, whole.shape[0] // count, whole.shape[1]) for whole in wholes]
    blocks = [jnp.concatenate([part[hop] for part in cut], axis=0) for hop in range(count)]
    total = blocks[0]
    if count == 1:
        return total, total
    half = total.shape[0] // 2
    first = total
    move = lambda part, by: lax.ppermute(
        part.astype(BF16), axis, shift_pairs(count, by)
    ).astype(F32)
    right = left = None
    if count % 2 == 0:
        far = blocks[count // 2]
        right, left = move(far[:half], 1), move(far[half:], -1)
        first = right
    for hop in range((count - 1) // 2, 0, -1):
        ahead, behind = blocks[hop], blocks[count - hop]
        if right is not None and right.shape[0] == half:
            ahead = jnp.concatenate([ahead[:half] + right, ahead[half:]], axis=0)
            behind = jnp.concatenate([behind[:half], behind[half:] + left], axis=0)
        elif right is not None:
            ahead, behind = ahead + right, behind + left
        right, left = move(ahead, 1), move(behind, -1)
    if right.shape[0] == half:
        return total + jnp.concatenate([right, left], axis=0), first
    return total + right + left, first


def hand_out(blocks, axis, by):
    count = lax.axis_size(axis)
    return [blocks[0]] + [
        lax.ppermute(blocks[hop], axis, shift_pairs(count, hop * by)) for hop in range(1, count)
    ]


def exchange(whole, axis):
    count = lax.axis_size(axis)
    me = lax.axis_index(axis)
    result = put_block(jnp.zeros(whole.shape, whole.dtype), take_block(whole, me), me)
    for hop in range(1, count):
        moved = lax.ppermute(
            take_block(whole, (me + hop) % count), axis, shift_pairs(count, hop)
        )
        result = put_block(result, moved, (me - hop) % count)
    return result


def after(values, *others):
    return lax.optimization_barrier((values, *others))[0]


def sum_everywhere(values):
    for axis in ("dp", "seq"):
        count = lax.axis_size(axis)
        if count & (count - 1):
            values = lax.psum(values, axis)
            continue
        mask = 1
        while mask < count:
            values = values + lax.ppermute(values, axis, swap_pairs(count, mask))
            mask *= 2
    return values


def round_up(size, step):
    return (size + step - 1) // step * step


def rms_parts(values):
    scale = lax.rsqrt(jnp.mean(values * values, axis=-1, keepdims=True) + 1e-05)
    return values * scale, scale


def rms_back(unit, scale, gain, adjoint):
    scaled = adjoint * gain
    return scale * (scaled - unit * jnp.mean(scaled * unit, axis=-1, keepdims=True))


def dot(left, right):
    return jnp.dot(left, right, preferred_element_type=F32)


def dot_nt(left, right):
    return jnp.einsum("tc,dc->td", left, right, preferred_element_type=F32)


def dot_tn(left, right):
    return jnp.einsum("tr,tc->rc", left, right, preferred_element_type=F32)


def by_heads(weight, ns):
    return jnp.swapaxes(weight.reshape(weight.shape[0], ns, weight.shape[1] // ns), 0, 1)


def pad_last(values, size):
    if values.shape[-1] == size:
        return values
    return jnp.pad(values, [(0, 0)] * (values.ndim - 1) + [(0, size - values.shape[-1])])


def hidden_out(weight, nd, ns, padded):
    rows, hidden = weight.shape
    block = hidden // (nd * ns)
    parts = jnp.transpose(weight.reshape(rows, nd, ns, block), (2, 0, 1, 3))
    return pad_last(parts.reshape(ns, rows, nd * block), padded)


def hidden_back(parts, nd, hidden):
    ns, rows, _ = parts.shape
    block = hidden // (nd * ns)
    kept = parts[:, :, : nd * block].reshape(ns, rows, nd, block)
    return jnp.transpose(kept, (1, 2, 0, 3)).reshape(rows, hidden)


def shards(
    inputs,
    cotangent,
    query_proj,
    key_proj,
    value_proj,
    gate_proj,
    rate_proj,
    output_proj,
    ffn_gate,
    ffn_up,
    ffn_down,
    mixer_gain,
    ffn_gain,
    query_filter,
    key_filter,
    value_filter,
    decay_log,
    step_bias,
    head_gain,
):
    seqs, piece, width = inputs.shape
    ns, nd = lax.axis_size("seq"), lax.axis_size("dp")
    me = lax.axis_index("seq")
    heads = H // ns
    kq, kv = heads * DK, heads * DV
    own = seqs * piece
    tokens = own * ns
    rows = query_proj.shape[0]
    hidden = ffn_gate.shape[1]
    hidden_own = hidden // ns
    padded = round_up(hidden_own, LANES)

    flat_in = inputs.reshape(own, width)
    flat_cot = cotangent.reshape(own, width)
    mixer_local = jnp.concatenate(
        [by_heads(w, ns) for w in (query_proj, key_proj, value_proj, gate_proj)]
        + [pad_last(by_heads(rate_proj, ns), LANES)],
        axis=2,
    )
    mixer_width = mixer_local.shape[2]
    ffn_local = jnp.concatenate(
        [hidden_out(ffn_gate, nd, ns, padded), hidden_out(ffn_up, nd, ns, padded)], axis=2
    )
    out_local = jnp.broadcast_to(output_proj.reshape(1, rows, -1), (ns, rows, output_proj.size // rows))
    near = near_pieces(flat_in, "seq")
    mixer_rows = exchange(mixer_local, "seq").reshape(ns * rows, mixer_width)
    mixer_rows, near = lax.optimization_barrier((mixer_rows, near))
    mixer_weight = lax.all_gather(mixer_rows, "dp", axis=0, tiled=True)
    all_in = ring_gather(flat_in, "seq", near)
    shared = exchange(after(jnp.concatenate([ffn_local, out_local], axis=2), near), "seq")
    out_rows = ns * output_proj.shape[0]
    out_here = shared[:, :, 2 * padded :].reshape(out_rows, width)
    down_rows = ffn_down.shape[0]
    spare = jnp.zeros((-(out_rows + down_rows) % 16, width), BF16)
    both = jnp.concatenate([out_here, ffn_down, spare], axis=0)
    both = lax.all_gather(both, "dp", axis=0, tiled=False)
    out_weight = both[:, :out_rows].reshape(ns, kv, width)
    turned = jnp.concatenate([take_block(out_weight, (me - hop) % ns) for hop in range(ns)], axis=0)
    down_weight = both[:, out_rows : out_rows + down_rows].reshape(hidden_own, width)
    down_weight = jnp.pad(down_weight, ((0, padded - hidden_own), (0, 0)))
    ffn_rows = shared[:, :, : 2 * padded].reshape(ns * rows, 2 * padded)
    ffn_weight = lax.all_gather(ffn_rows, "dp", axis=0, tiled=True)

    chunk_rows = min(CHUNK, piece)
    per_piece = piece // chunk_rows
    order = jnp.stack(
        [
            (((part - me) % ns) * seqs + row) * per_piece + within
            for row in range(seqs)
            for part in range(ns)
            for within in range(per_piece)
        ]
    ).astype(jnp.int32)
    unit_in, scale_in = rms_parts(all_in.astype(F32))
    normed = (unit_in * mixer_gain).astype(BF16)
    projected = dot(normed, mixer_weight).astype(BF16)
    own_cols = lambda table, size: lax.dynamic_slice_in_dim(table, me * size, size, 1)
    filters = jnp.concatenate(
        [own_cols(query_filter, kq), own_cols(key_filter, kq), own_cols(value_filter, kv)], axis=1
    )
    own_decay = jnp.exp(lax.dynamic_slice_in_dim(decay_log, me * heads, heads, 0))
    own_bias = lax.dynamic_slice_in_dim(step_bias, me * heads, heads, 0)
    spread = lambda values: pad_last(
        jnp.stack([jnp.zeros_like(values), values], axis=1).reshape(1, 2 * heads), LANES
    )
    side = jnp.concatenate(
        [spread(own_decay), spread(own_bias), jnp.zeros((6, LANES), F32)], axis=0
    )
    gain_row = head_gain.reshape(1, DV)
    mixed, *saved = mixer_forward(
        projected, filters, side, gain_row, order, heads, seqs, chunk_rows
    )
    cot_near = near_pieces(after(flat_cot, projected), "seq")
    mixed, cot_near = lax.optimization_barrier((mixed, cot_near))
    all_cot = ring_gather(flat_cot, "seq", cot_near)
    mixed_parts = hand_out(mixed.reshape(ns, own, kv), "seq", 1)
    mixed_low = jnp.concatenate(mixed_parts, axis=1)

    middle = flat_in.astype(F32) + dot(mixed_low, turned)
    unit_two, scale_two = rms_parts(middle)
    second_all = ring_gather((unit_two * ffn_gain).astype(BF16), "seq")
    hidden_both = dot(second_all, ffn_weight)
    hidden_gate, hidden_up = hidden_both[:, :padded], hidden_both[:, padded:]
    gate_sig = jax.nn.sigmoid(hidden_gate)
    gate_silu = hidden_gate * gate_sig
    active = (gate_silu * hidden_up).astype(BF16)
    adj_act = dot_nt(all_cot, down_weight)
    adj_gate = adj_act * hidden_up * silu_slope(hidden_gate, gate_sig)
    adj_both = jnp.concatenate(
        [adj_gate.astype(BF16), (adj_act * gate_silu).astype(BF16)], axis=1
    )
    adj_partial_two = dot_nt(adj_both, ffn_weight)
    adj_second, first_in = ring_reduce([adj_partial_two], "seq")
    scatter = lambda grad: lax.psum_scatter(
        grad.astype(BF16), "dp", scatter_dimension=0, tiled=True
    )
    active_late, adj_both_late = after((active, adj_both), first_in)
    grad_ffn = dot_tn(second_all, adj_both_late).astype(BF16)
    ffn_sums = scatter(grad_ffn)
    adj_second = after(adj_second, grad_ffn)
    grad_down = dot_tn(active_late, all_cot)[:hidden_own].astype(BF16)

    gain_two = jnp.sum(adj_second * unit_two, axis=0)
    adj_middle = flat_cot.astype(F32) + rms_back(unit_two, scale_two, ffn_gain, adj_second)
    attn_low = adj_middle.astype(BF16)
    attn_near = near_pieces(attn_low, "seq")
    active_late = after(active, attn_low)
    block_parts = dot(active_late, down_weight)
    attn_all = ring_gather(attn_low, "seq", attn_near)
    adj_heads = dot_nt(attn_all, take_block(out_weight, me)).astype(BF16)
    grad_out = dot_tn(mixed, attn_all).astype(BF16)
    head_rows = kv // nd
    spare = jnp.zeros((nd, -(head_rows + down_rows) % 16, width), BF16)
    both_grads = jnp.concatenate(
        [
            grad_out.reshape(nd, head_rows, width),
            grad_down.reshape(nd, down_rows, width),
            spare,
        ],
        axis=1,
    ).reshape(-1, width)
    both_sums = scatter(both_grads)
    adj_heads = after(adj_heads, both_grads, ffn_sums)
    down_out = both_sums[head_rows : head_rows + down_rows]
    owners = [
        (place * ns + part, part * nd + place) for place in range(nd) for part in range(ns)
    ]
    out_out = lax.ppermute(both_sums[:head_rows], ("dp", "seq"), owners)

    adj_projected, filter_sum, side_sum, gain_sum = mixer_backward(
        projected, filters, side, gain_row, adj_heads, saved, order, heads, seqs, chunk_rows
    )
    grad_mixer = dot_tn(normed, adj_projected).astype(BF16)
    mixer_sums = scatter(after(grad_mixer, both_sums))
    adj_partial = dot_nt(after(adj_projected, grad_mixer), mixer_weight)
    gain_one = jnp.sum(adj_partial * unit_in, axis=0)
    reduced, _ = ring_reduce([adj_partial, block_parts], "seq")
    adj_normed, block_sum = reduced[:own], reduced[own:]
    shared = jnp.concatenate(
        [mixer_sums.reshape(ns, rows, -1), ffn_sums.reshape(ns, rows, -1)], axis=2
    )
    shared = exchange(shared, "seq")
    shared, adj_normed, block_sum = lax.optimization_barrier((shared, adj_normed, block_sum))
    mixer_parts, ffn_parts = shared[:, :, :-2 * padded], shared[:, :, -2 * padded:]
    block_out = (middle + block_sum).astype(BF16).reshape(inputs.shape)
    ffngate_out = hidden_back(ffn_parts[:, :, :padded], nd, hidden)
    ffnup_out = hidden_back(ffn_parts[:, :, padded:], nd, hidden)
    whole_rows = lambda parts: jnp.swapaxes(parts, 0, 1).reshape(rows, -1)
    query_out = whole_rows(mixer_parts[:, :, :kq])
    key_out = whole_rows(mixer_parts[:, :, kq : 2 * kq])
    value_out = whole_rows(mixer_parts[:, :, 2 * kq : 2 * kq + kv])
    gate_out = whole_rows(mixer_parts[:, :, 2 * kq + kv : 2 * kq + 2 * kv])
    rate_at = 2 * kq + 2 * kv
    rate_out = whole_rows(mixer_parts[:, :, rate_at : rate_at + 2 * heads])

    unit_one, scale_one = rms_parts(flat_in.astype(F32))
    grad_inputs = (
        (adj_middle + rms_back(unit_one, scale_one, mixer_gain, adj_normed))
        .astype(BF16)
        .reshape(inputs.shape)
    )

    def place(own_part, table, size):
        return lax.dynamic_update_slice_in_dim(
            jnp.zeros(table.shape, F32), own_part, me * size, table.ndim - 1
        )

    small = (
        gain_one,
        gain_two,
        place(filter_sum[:, :kq], query_filter, kq),
        place(filter_sum[:, kq : 2 * kq], key_filter, kq),
        place(filter_sum[:, 2 * kq :], value_filter, kv),
        place(side_sum[0, 1 : 2 * heads : 2], decay_log, heads),
        place(side_sum[1, 1 : 2 * heads : 2], step_bias, heads),
        gain_sum.reshape(DV),
    )
    packed = jnp.concatenate([pad_last(part.reshape(-1), round_up(part.size, LANES)) for part in small])
    packed = sum_everywhere(packed.reshape(-1, LANES)).astype(BF16).reshape(-1)
    outs = []
    at = 0
    for part in small:
        outs.append(packed[at : at + part.size].reshape(part.shape))
        at += round_up(part.size, LANES)
    return (
        block_out,
        grad_inputs,
        query_out,
        key_out,
        value_out,
        gate_out,
        rate_out,
        out_out,
        ffngate_out,
        ffnup_out,
        down_out,
        *outs,
    )


def solution(mesh):
    tokens = P("dp", "seq", None)
    weight = P(("dp", "seq"), None)
    specs = (tokens,) * 2 + (weight,) * 9 + (P(),) * 8
    return jax.shard_map(shards, mesh=mesh, in_specs=specs, out_specs=specs, check_vma=False)
```
